32 devices in a mesh: wide: 16 (over z, y, core), narrow: 2 (over x).
Axes of the slice: x: 2, y: 2, z: 4, core: 2. Of those that a mesh axis runs over, the one named last changes fastest.
Arguments:
- tokens: bfloat16 [32768, 768], P(('wide', 'narrow')), may hold values from -6 to 6
- kept_patches: int32 [256, 128], P(('wide', 'narrow')), may hold values from 0 to 511, as said below
- resolution: int32 [256], P(('wide', 'narrow')), may hold values from 0 to 1, as said below
- position_table: bfloat16 [640, 768], replicated, may hold values from -4 to 4
- norm_one_gain: bfloat16 [768], replicated, may hold values from 0.25 to 1.75
- norm_one_shift: bfloat16 [768], replicated, may hold values from -3 to 3
- project_weight: bfloat16 [768, 2304], replicated, may hold values from -0.21875 to 0.21875
- query_bias: bfloat16 [768], replicated, may hold values from -3 to 3
- value_bias: bfloat16 [768], replicated, may hold values from -3 to 3
- output_weight: bfloat16 [768, 768], replicated, may hold values from -0.875 to 0.875
- output_bias: bfloat16 [768], replicated, may hold values from -3 to 3
- norm_two_gain: bfloat16 [768], replicated, may hold values from 0.25 to 1.75
- norm_two_shift: bfloat16 [768], replicated, may hold values from -3 to 3
- expand_weight: bfloat16 [768, 3072], replicated, may hold values from -0.21875 to 0.21875
- expand_bias: bfloat16 [3072], replicated, may hold values from -3 to 3
- reduce_weight: bfloat16 [3072, 768], replicated, may hold values from -0.109375 to 0.109375
- reduce_bias: bfloat16 [768], replicated, may hold values from -3 to 3
- cotangent: bfloat16 [32768, 768], P(('wide', 'narrow')), may hold values from -6 to 6
Outputs:
- layer_output: bfloat16 [32768, 768], P(('wide', 'narrow'))
- token_gradient: bfloat16 [32768, 768], P(('wide', 'narrow'))
- position_gradient: float32 [640, 768], replicated
- norm_one_gain_gradient: float32 [768], replicated
- norm_one_shift_gradient: float32 [768], replicated
- project_weight_gradient: float32 [768, 2304], replicated
- query_bias_gradient: float32 [768], replicated
- value_bias_gradient: float32 [768], replicated
- output_weight_gradient: float32 [768, 768], replicated
- output_bias_gradient: float32 [768], replicated
- norm_two_gain_gradient: float32 [768], replicated
- norm_two_shift_gradient: float32 [768], replicated
- expand_weight_gradient: float32 [768, 3072], replicated
- expand_bias_gradient: float32 [3072], replicated
- reduce_weight_gradient: float32 [3072, 768], replicated
- reduce_bias_gradient: float32 [768], replicated
The draws below stay inside these ranges and needn't reach their ends.
Inputs may be any that keep to these rules, and one draw needn't show every extreme that they name: `kept_patches`: in a group with resolution 1 the entries are 128 distinct patches of one fine sample. In a group with resolution 0 the group holds 4 coarse samples: for each s the rows with entry // 128 = s are 32 distinct patches of that sample. `resolution`: the same on all 8 groups of one device.
All inputs are finite; a program needn't handle non-finite values.
Results may differ from the reference program's by a relative error of at most 0.012.
Values sent between devices are 32-bit elements; how exact they have to be, the bound alone decides.
No kernel may reach another device: no remote copies, remote signals or barrier semaphores. Data moves between devices by JAX's collectives and lax.ppermute only.
A program may use at most 192 MiB of HBM per device.

```python
import math
import jax
import jax.numpy as jnp
from jax import lax

D = 768
FF = 3072
HEADS = 12
PATCH_LO = 128
PATCH_HI = 512
VIS_LO = 32
GROUP = 128
G_DEV = 8
GROUPS = 256
ROWS = 32768
PLACES = 640


def draw_levels(key):
    device_count = GROUPS // G_DEV
    per_device = jax.random.randint(jax.random.fold_in(key, 11), (device_count,), 0, 2)
    return jnp.repeat(per_device, G_DEV).astype(jnp.int32)


def draw_resolution(key, part):
    return draw_levels(key)


def draw_kept_patches(key, part):
    levels = draw_levels(key)
    sample_count = GROUP // VIS_LO
    fine_keys = jax.random.split(jax.random.fold_in(key, 23), GROUPS)
    fine_rows = jax.vmap(lambda one_key: jax.random.permutation(one_key, PATCH_HI)[:GROUP])(fine_keys)
    coarse_keys = jax.random.split(jax.random.fold_in(key, 37), GROUPS * sample_count)
    coarse_rows = jax.vmap(lambda one_key: jax.random.permutation(one_key, PATCH_LO)[:VIS_LO])(coarse_keys)
    coarse_rows = coarse_rows.reshape(GROUPS, sample_count, VIS_LO)
    coarse_rows = coarse_rows + (jnp.arange(sample_count, dtype=jnp.int32) * PATCH_LO)[None, :, None]
    coarse_rows = coarse_rows.reshape(GROUPS, GROUP)
    return jnp.where(levels[:, None] == 1, fine_rows, coarse_rows).astype(jnp.int32)


def block_levels(stream_key, dims, cuts, least, high):
    def one(dim, parts):
        heights = jax.random.uniform(jax.random.fold_in(jax.random.fold_in(stream_key, 6), dim), (parts,), jnp.float32, least / len(cuts), high / len(cuts))
        return jnp.repeat(jnp.exp(heights), dims[dim] // parts).reshape((-1,) + (1,) * (len(dims) - dim - 1))

    factor_of = one(*cuts[0])
    for cut in cuts[1:]:
        factor_of = factor_of * one(*cut)
    return factor_of


def noise(rng, shape, width, limit, cuts=(), kind=jnp.bfloat16):
    values = width * jax.random.normal(rng, shape, jnp.float32)
    if cuts:
        values = values * block_levels(rng, shape, cuts, -0.22, 0.18)
    return jnp.clip(values, -limit, limit).astype(kind)


def setup_inputs(seed: int = 0) -> dict:
    key_list = jax.random.split(jax.random.key(seed), 19)
    tokens = noise(key_list[0], (ROWS, D), 1.0, 6.0, ((0, 32),))
    kept_patches = draw_kept_patches(jax.random.fold_in(key_list[18], 71), 0)
    resolution = draw_resolution(jax.random.fold_in(key_list[18], 71), 0)
    position_table = noise(key_list[3], (PLACES, D), 0.5, 4.0)
    norm_one_gain = jnp.clip(1.0 + 0.15 * jax.random.normal(key_list[4], (D,), jnp.float32), 0.25, 1.75).astype(jnp.bfloat16)
    norm_one_shift = noise(key_list[5], (D,), 0.3, 3.0)
    project_weight = noise(key_list[6], (D, 3 * D), D ** -0.5, 0.21875)
    query_bias = noise(key_list[7], (D,), 0.3, 3.0)
    value_bias = noise(key_list[8], (D,), 0.5, 3.0)
    output_weight = noise(key_list[9], (D, D), (D // 16) ** -0.5, 0.875)
    output_bias = noise(key_list[10], (D,), 0.3, 3.0)
    norm_two_gain = jnp.clip(1.0 + 0.15 * jax.random.normal(key_list[11], (D,), jnp.float32), 0.25, 1.75).astype(jnp.bfloat16)
    norm_two_shift = noise(key_list[12], (D,), 0.3, 3.0)
    expand_weight = noise(key_list[13], (D, FF), D ** -0.5, 0.21875)
    expand_bias = noise(key_list[14], (FF,), 0.5, 3.0)
    reduce_weight = noise(key_list[15], (FF, D), FF ** -0.5, 0.109375)
    reduce_bias = noise(key_list[16], (D,), 0.3, 3.0)
    cotangent = noise(key_list[17], (ROWS, D), 1.0, 6.0, ((0, 32),))
    return {"tokens": tokens, "kept_patches": kept_patches, "resolution": resolution, "position_table": position_table, "norm_one_gain": norm_one_gain, "norm_one_shift": norm_one_shift, "project_weight": project_weight, "query_bias": query_bias, "value_bias": value_bias, "output_weight": output_weight, "output_bias": output_bias, "norm_two_gain": norm_two_gain, "norm_two_shift": norm_two_shift, "expand_weight": expand_weight, "expand_bias": expand_bias, "reduce_weight": reduce_weight, "reduce_bias": reduce_bias, "cotangent": cotangent}


@jax.custom_vjp
def low(v):
    return lax.optimization_barrier(v.astype(jnp.bfloat16)).astype(jnp.float32)

@jax.custom_vjp
def low_back(v):
    return v

def low_keep(v):
    return (low(v), None)

def low_pass(kept, grad):
    return (grad,)

def back_keep(v):
    return (v, None)

def back_low(kept, grad):
    return (low(grad),)
low.defvjp(low_keep, low_pass)
low_back.defvjp(back_keep, back_low)
epsilon = 1e-06
big_negative = -1e+30

def layer_norm(stream, norm_gain, norm_shift):
    centre = stream - lax.optimization_barrier(jnp.mean(stream, axis=-1, keepdims=True))
    variance = lax.optimization_barrier(jnp.mean(centre * centre, axis=-1, keepdims=True))
    return centre * lax.rsqrt(variance + epsilon) * norm_gain + norm_shift

def product(first, second):
    return jnp.dot(first, second, precision=lax.Precision.HIGHEST)

def layer_forward(parameters, tokens_block, place_block, sample_block):
    position_table, norm_one_gain, norm_one_shift, project_weight, query_bias, value_bias, output_weight, output_bias, norm_two_gain, norm_two_shift, expand_weight, expand_bias, reduce_weight, reduce_bias = parameters
    blocks, row_count, model_width = tokens_block.shape
    head_width = model_width // HEADS
    stream_in = tokens_block + position_table[place_block]
    normed_one = low(layer_norm(stream_in, norm_one_gain, norm_one_shift))
    joined_bias = jnp.concatenate([query_bias, jnp.zeros_like(query_bias), value_bias])
    projected = low_back(low(product(normed_one, project_weight) + joined_bias))
    projected = projected.reshape(blocks, row_count, 3, HEADS, head_width)
    queries = projected[:, :, 0]
    keys_all = projected[:, :, 1]
    values = projected[:, :, 2]
    score_scale = head_width ** (-0.5)
    scores = low_back(jnp.einsum('bqhd,bkhd->bhqk', queries, keys_all, precision=lax.Precision.HIGHEST) * score_scale)
    same_sample = (sample_block[:, :, None] == sample_block[:, None, :])[:, None]
    weights = low(jax.nn.softmax(jnp.where(same_sample, scores, big_negative), axis=-1))
    heads_out = jnp.einsum('bhqk,bkhd->bqhd', weights, values, precision=lax.Precision.HIGHEST)
    heads_out = low_back(low(heads_out.reshape(blocks, row_count, model_width)))
    stream_mid = stream_in + low_back(product(heads_out, output_weight) + output_bias)
    normed_two = low(layer_norm(stream_mid, norm_two_gain, norm_two_shift))
    hidden_pre = low_back(product(normed_two, expand_weight) + expand_bias)
    hidden = low(jax.nn.gelu(hidden_pre, approximate=False))
    return stream_mid + product(hidden, reduce_weight) + reduce_bias

def reference(tokens, kept_patches, resolution, position_table, norm_one_gain, norm_one_shift, project_weight, query_bias, value_bias, output_weight, output_bias, norm_two_gain, norm_two_shift, expand_weight, expand_bias, reduce_weight, reduce_bias, cotangent):
    group_count = kept_patches.shape[0]
    model_width = tokens.shape[1]
    fine_grid = resolution[:, None] == 1
    place_index = jnp.where(fine_grid, PATCH_LO + kept_patches, kept_patches % PATCH_LO).astype(jnp.int32)
    sample_index = jnp.where(fine_grid, 0, kept_patches // PATCH_LO).astype(jnp.int32)
    parameters = tuple((weight.astype(jnp.float32) for weight in (position_table, norm_one_gain, norm_one_shift, project_weight, query_bias, value_bias, output_weight, output_bias, norm_two_gain, norm_two_shift, expand_weight, expand_bias, reduce_weight, reduce_bias)))
    per_step = math.gcd(group_count, 32)
    step_count = group_count // per_step
    token_blocks = tokens.astype(jnp.float32).reshape(step_count, per_step, GROUP, model_width)
    cotangent_blocks = cotangent.astype(jnp.float32).reshape(step_count, per_step, GROUP, model_width)
    place_blocks = place_index.reshape(step_count, per_step, GROUP)
    sample_blocks = sample_index.reshape(step_count, per_step, GROUP)

    def one_step(totals, inputs):
        token_block, cotangent_block, place_block, sample_block = inputs

        def forward(weights_all, stream):
            return layer_forward(weights_all, stream, place_block, sample_block)
        result, pullback = jax.vjp(forward, parameters, token_block)
        weight_grads, stream_grad = pullback(cotangent_block)
        totals = jax.tree.map(jnp.add, totals, weight_grads)
        return (totals, (result.astype(jnp.bfloat16), stream_grad.astype(jnp.bfloat16)))
    zeros_start = jax.tree.map(jnp.zeros_like, parameters)
    totals, (outputs, token_grads) = lax.scan(one_step, zeros_start, (token_blocks, cotangent_blocks, place_blocks, sample_blocks))
    position_gradient, norm_one_gain_gradient, norm_one_shift_gradient, project_weight_gradient, query_bias_gradient, value_bias_gradient, output_weight_gradient, output_bias_gradient, norm_two_gain_gradient, norm_two_shift_gradient, expand_weight_gradient, expand_bias_gradient, reduce_weight_gradient, reduce_bias_gradient = totals
    return (outputs.reshape(-1, model_width), token_grads.reshape(-1, model_width), position_gradient, norm_one_gain_gradient, norm_one_shift_gradient, project_weight_gradient, query_bias_gradient, value_bias_gradient, output_weight_gradient, output_bias_gradient, norm_two_gain_gradient, norm_two_shift_gradient, expand_weight_gradient, expand_bias_gradient, reduce_weight_gradient, reduce_bias_gradient)
```

```python
from functools import partial

import jax
import jax.numpy as jnp
from jax import lax
from jax.sharding import PartitionSpec as P

HEADS = 12
PATCH_LO = 128


epsilon = 1e-06
big_negative = -1e30


def norm_forward(stream, norm_gain, norm_shift):
    centre = stream - jnp.mean(stream, axis=-1, keepdims=True)
    inverse = lax.rsqrt(jnp.mean(centre * centre, axis=-1, keepdims=True) + epsilon)
    normed = centre * inverse
    return (normed, inverse, normed * norm_gain + norm_shift)


def norm_backward(upstream, normed, inverse, norm_gain):
    scaled = upstream * norm_gain
    inner = jnp.mean(scaled * normed, axis=-1, keepdims=True)
    stream_gradient = inverse * (scaled - jnp.mean(scaled, axis=-1, keepdims=True) - normed * inner)
    return (stream_gradient, jnp.sum(upstream * normed, axis=0), jnp.sum(upstream, axis=0))


def body(
    tokens,
    kept_patches,
    resolution,
    position_table,
    norm_one_gain,
    norm_one_shift,
    project_weight,
    query_bias,
    value_bias,
    output_weight,
    output_bias,
    norm_two_gain,
    norm_two_shift,
    expand_weight,
    expand_bias,
    reduce_weight,
    reduce_bias,
    cotangent,
):
    f32 = jnp.float32
    bf16 = jnp.bfloat16
    group_count, group_rows = kept_patches.shape
    model_width = tokens.shape[1]
    head_width = model_width // HEADS
    score_scale = head_width ** (-0.5)
    fine_grid = resolution[:, None] == 1
    place_index = jnp.where(fine_grid, PATCH_LO + kept_patches, kept_patches % PATCH_LO).reshape(-1)
    sample_index = jnp.where(fine_grid, 0, kept_patches // PATCH_LO)
    same_sample = (sample_index[:, :, None] == sample_index[:, None, :])[:, None]

    def split_heads(columns):
        return columns.reshape(group_count, group_rows, HEADS, head_width)

    stream_in = tokens.astype(f32) + jnp.take(position_table, place_index, axis=0).astype(f32)
    one_gain = norm_one_gain.astype(f32)
    normed_one, inverse_one, affine_one = norm_forward(
        stream_in, one_gain, norm_one_shift.astype(f32)
    )
    first_low = affine_one.astype(bf16)
    joined_bias = jnp.concatenate([query_bias, jnp.zeros_like(query_bias), value_bias]).astype(f32)
    projected = (
        jnp.dot(first_low, project_weight, preferred_element_type=f32) + joined_bias
    ).astype(bf16)
    queries = split_heads(projected[:, :model_width])
    keys_all = split_heads(projected[:, model_width : 2 * model_width])
    values = split_heads(projected[:, 2 * model_width :])

    def masked_scores():
        raw_scores = (
            jnp.einsum("gqhd,gkhd->ghqk", queries, keys_all, preferred_element_type=f32)
            * score_scale
        )
        return jnp.where(same_sample, raw_scores, big_negative)

    scores = masked_scores()
    top_score = jnp.max(scores, axis=-1, keepdims=True)
    exponent = jnp.exp(scores - top_score)
    total = jnp.sum(exponent, axis=-1, keepdims=True)
    softmax_weights = exponent / total
    log_total = top_score + jnp.log(total)
    heads_out = (
        jnp.einsum(
            "ghqk,gkhd->gqhd", softmax_weights.astype(bf16), values, preferred_element_type=f32
        )
        .reshape(-1, model_width)
        .astype(bf16)
    )
    stream_mid = stream_in + (
        jnp.dot(heads_out, output_weight, preferred_element_type=f32) + output_bias.astype(f32)
    )
    two_gain = norm_two_gain.astype(f32)
    normed_two, inverse_two, affine_two = norm_forward(
        stream_mid, two_gain, norm_two_shift.astype(f32)
    )
    second_low = affine_two.astype(bf16)
    hidden_pre = jnp.dot(
        second_low, expand_weight, preferred_element_type=f32
    ) + expand_bias.astype(f32)
    hidden, gelu_back = jax.vjp(partial(jax.nn.gelu, approximate=False), hidden_pre)
    hidden_low = hidden.astype(bf16)
    layer_output = (
        stream_mid
        + (jnp.dot(hidden_low, reduce_weight, preferred_element_type=f32) + reduce_bias.astype(f32))
    ).astype(bf16)
    out_gradient = cotangent.astype(f32)
    reduce_weight_gradient = jnp.einsum(
        "rf,rd->fd", hidden_low, cotangent, preferred_element_type=f32
    )
    reduce_bias_gradient = jnp.sum(out_gradient, axis=0)
    hidden_gradient = jnp.einsum("rd,fd->rf", cotangent, reduce_weight, preferred_element_type=f32)
    pre_gradient = gelu_back(hidden_gradient)[0].astype(bf16)
    expand_bias_gradient = jnp.sum(pre_gradient.astype(f32), axis=0)
    expand_weight_gradient = jnp.einsum(
        "rd,rf->df", second_low, pre_gradient, preferred_element_type=f32
    )
    second_gradient = jnp.einsum(
        "rf,df->rd", pre_gradient, expand_weight, preferred_element_type=f32
    )
    mid_from_norm, norm_two_gain_gradient, norm_two_shift_gradient = norm_backward(
        second_gradient, normed_two, inverse_two, two_gain
    )
    mid_gradient = out_gradient + mid_from_norm
    branch_gradient = mid_gradient.astype(bf16)
    output_bias_gradient = jnp.sum(branch_gradient.astype(f32), axis=0)
    output_weight_gradient = jnp.einsum(
        "re,rd->ed", heads_out, branch_gradient, preferred_element_type=f32
    )
    heads_gradient = split_heads(
        jnp.einsum("rd,ed->re", branch_gradient, output_weight, preferred_element_type=f32).astype(
            bf16
        )
    )
    again_weights = jnp.exp(masked_scores() - log_total)
    weight_gradient = jnp.einsum(
        "gqhd,gkhd->ghqk", heads_gradient, values, preferred_element_type=f32
    )
    value_gradient = jnp.einsum(
        "ghqk,gqhd->gkhd", again_weights.astype(bf16), heads_gradient, preferred_element_type=f32
    )
    row_inner = jnp.sum(weight_gradient * again_weights, axis=-1, keepdims=True)
    score_gradient = (again_weights * (weight_gradient - row_inner)).astype(bf16)
    query_gradient = (
        jnp.einsum("ghqk,gkhd->gqhd", score_gradient, keys_all, preferred_element_type=f32)
        * score_scale
    )
    key_gradient = (
        jnp.einsum("ghqk,gqhd->gkhd", score_gradient, queries, preferred_element_type=f32)
        * score_scale
    )
    projected_gradient = jnp.concatenate(
        [
            query_gradient.reshape(-1, model_width),
            key_gradient.reshape(-1, model_width),
            value_gradient.reshape(-1, model_width),
        ],
        axis=1,
    ).astype(bf16)
    query_bias_gradient = jnp.sum(projected_gradient[:, :model_width].astype(f32), axis=0)
    value_bias_gradient = jnp.sum(projected_gradient[:, 2 * model_width :].astype(f32), axis=0)
    project_weight_gradient = jnp.einsum(
        "rd,re->de", first_low, projected_gradient, preferred_element_type=f32
    )
    first_gradient = jnp.einsum(
        "re,de->rd", projected_gradient, project_weight, preferred_element_type=f32
    )
    in_from_norm, norm_one_gain_gradient, norm_one_shift_gradient = norm_backward(
        first_gradient, normed_one, inverse_one, one_gain
    )
    in_gradient = mid_gradient + in_from_norm
    token_gradient = in_gradient.astype(bf16)
    position_gradient = jax.ops.segment_sum(
        in_gradient, place_index, num_segments=position_table.shape[0]
    )
    every = ("wide", "narrow")
    small = jnp.concatenate(
        [
            norm_one_gain_gradient,
            norm_one_shift_gradient,
            query_bias_gradient,
            value_bias_gradient,
            output_bias_gradient,
            norm_two_gain_gradient,
            norm_two_shift_gradient,
            reduce_bias_gradient,
            expand_bias_gradient,
            jnp.zeros((4 * model_width,), f32),
        ]
    ).reshape(-1, model_width)
    places = position_table.shape[0]
    reduce_weight_gradient = lax.psum(reduce_weight_gradient, every)
    expand_weight_gradient, reduce_weight_gradient = lax.optimization_barrier(
        (expand_weight_gradient, reduce_weight_gradient)
    )
    expand_weight_gradient = lax.psum(expand_weight_gradient, every)
    project_weight_gradient, expand_weight_gradient = lax.optimization_barrier(
        (project_weight_gradient, expand_weight_gradient)
    )
    project_weight_gradient = lax.psum(project_weight_gradient, every)
    mixed, project_weight_gradient = lax.optimization_barrier(
        (
            jnp.concatenate([position_gradient, small, output_weight_gradient]),
            project_weight_gradient,
        )
    )
    mixed = lax.psum(mixed, every)
    position_gradient = mixed[:places]
    (
        norm_one_gain_gradient,
        norm_one_shift_gradient,
        query_bias_gradient,
        value_bias_gradient,
        output_bias_gradient,
        norm_two_gain_gradient,
        norm_two_shift_gradient,
        reduce_bias_gradient,
    ) = (mixed[places + k] for k in range(8))
    expand_bias_gradient = mixed[places + 8 : places + 12].reshape(-1)
    output_weight_gradient = mixed[places + 16 :]
    return (
        layer_output,
        token_gradient,
        position_gradient,
        norm_one_gain_gradient,
        norm_one_shift_gradient,
        project_weight_gradient,
        query_bias_gradient,
        value_bias_gradient,
        output_weight_gradient,
        output_bias_gradient,
        norm_two_gain_gradient,
        norm_two_shift_gradient,
        expand_weight_gradient,
        expand_bias_gradient,
        reduce_weight_gradient,
        reduce_bias_gradient,
    )


def solution(mesh):
    placed = (
        P(("wide", "narrow"), None),
        P(("wide", "narrow"), None),
        P(("wide", "narrow")),
        P(),
        P(),
        P(),
        P(),
        P(),
        P(),
        P(),
        P(),
        P(),
        P(),
        P(),
        P(),
        P(),
        P(),
        P(("wide", "narrow"), None),
    )
    return jax.shard_map(
        body,
        mesh=mesh,
        in_specs=placed,
        out_specs=(
            P(("wide", "narrow"), None),
            P(("wide", "narrow"), None),
            P(),
            P(),
            P(),
            P(),
            P(),
            P(),
            P(),
            P(),
            P(),
            P(),
            P(),
            P(),
            P(),
            P(),
        ),
        check_vma=False,
    )
```

```python
import itertools

import jax
import jax.numpy as jnp
from jax import lax
from jax.experimental import pallas as pl
from jax.experimental.pallas import tpu as pltpu
from jax.sharding import Mesh, PartitionSpec as P

HEADS = 12
PATCH_LO = 128
BLOCK = 256
WIDE = 512
PLAN = "|a|b|a|b|ab||paq+mbpaqbmapqbmpaqb*pmaqpbampqbmpqmpqqmm"

SMALL = pl.CostEstimate(flops=1, transcendentals=0, bytes_accessed=1)

epsilon = 1e-06
big_negative = -1e30
f32 = jnp.float32
bf16 = jnp.bfloat16


AXES = ("z", "y", "c", "x")
CHIPS_FIRST = ("z", "y", "x", "c")


def pairs(sizes, target):
    found = []
    for here in itertools.product(*(range(n) for n in sizes)):
        there = target(*here)
        if there is not None:
            found.append((flat(sizes, here), flat(sizes, there)))
    return found


def flat(sizes, place):
    index = 0
    for n, k in zip(sizes, place):
        index = index * n + k
    return index


def send(value, sizes, target):
    return lax.ppermute(value, AXES, pairs(sizes, target))


def across_core(z, y, c, x):
    return (z, y, 1 - c, x)


def plane_one(z, y, c, x):
    return (z, y, c, 1 - x) if c == 0 else (z, 1 - y, c, x)


def plane_two(z, y, c, x):
    return (z, 1 - y, c, x) if c == 0 else (z, y, c, 1 - x)


def ends_in(z, y, c, x):
    return {0: (1, y, c, x), 3: (2, y, c, x)}.get(z)


def middle(z, y, c, x):
    return {1: (2, y, c, x), 2: (1, y, c, x)}.get(z)


def ends_out(z, y, c, x):
    return {1: (0, y, c, x), 2: (3, y, c, x)}.get(z)


def half(value, index):
    rows = value.shape[0] // 2
    return lax.dynamic_slice_in_dim(value, index * rows, rows, 0)


def join(own, other, index):
    return jnp.concatenate(
        [jnp.where(index == 0, own, other), jnp.where(index == 0, other, own)], axis=0
    )


class Order:
    def __init__(self, token):
        self.token = token

    def tie(self, *values):
        *values, self.token = lax.optimization_barrier((*values, self.token))
        return values[0] if len(values) == 1 else tuple(values)


def plane_first(parts, sizes):
    z, y, c, x = (lax.axis_index(axis) for axis in AXES)
    first = jnp.where(c == 0, x, y)
    second = jnp.where(c == 0, y, x)
    other = sum(half(part, 1 - c) for part in parts)
    came = yield other, across_core
    value = sum(half(part, c) for part in parts) + came
    came = yield half(value, 1 - first), plane_one
    value = half(value, first) + came
    came = yield half(value, 1 - second), plane_two
    value = half(value, second) + came
    value = value + (yield value, ends_in)
    value = value + (yield value, middle)
    came = yield value, ends_out
    value = jnp.where((z == 0) | (z == 3), came, value)
    value = join(value, (yield value, plane_two), second)
    value = join(value, (yield value, plane_one), first)
    came = yield value, across_core
    return value, came


class Sums:
    def __init__(self, sizes, order):
        self.sizes, self.order = sizes, order
        self.steps, self.flying, self.results = {}, {}, {}

    def begin(self, name, steps):
        self.steps[name] = steps
        self.post(name, next(steps))

    def post(self, name, step):
        value, target = step
        self.flying[name] = send(self.order.tie(value), self.sizes, target)

    def wait(self, *names):
        for name in names:
            came = self.order.tie(self.flying.pop(name))
            try:
                step = self.steps[name].send(came)
            except StopIteration as stop:
                self.results[name] = stop.value
            else:
                self.post(name, step)


def assemble(index, pairs, begin, rows, block):
    count = len(pairs)
    steps = rows // block
    lead = begin // block
    width = sum(own.shape[1] for own, _ in pairs)

    def kernel(where, *refs):
        mine = pl.program_id(0) == where[0]
        out = refs[-1]
        at = 0
        for own, other in zip(refs[:count], refs[count : 2 * count]):
            span = slice(at, at + own.shape[1])
            at += own.shape[1]

            @pl.when(mine)
            def _():
                out[:, span] = own[...]

            @pl.when(jnp.logical_not(mine))
            def _():
                out[:, span] = other[...]

    def own_map(h, i, where):
        return (lead + jnp.where(h == where[0], i, jnp.where(h == 0, 0, steps - 1)), 0)

    def other_map(h, i, where):
        return (lead + jnp.where(h == where[0], jnp.where(h == 0, 0, steps - 1), i), 0)

    return pl.pallas_call(
        kernel,
        name="assemble",
        grid_spec=pltpu.PrefetchScalarGridSpec(
            num_scalar_prefetch=1,
            grid=(2, steps),
            in_specs=[pl.BlockSpec((block, own.shape[1]), own_map) for own, _ in pairs]
            + [pl.BlockSpec((block, own.shape[1]), other_map) for own, _ in pairs],
            out_specs=pl.BlockSpec((block, width), lambda h, i, where: (h * steps + i, 0)),
        ),
        out_shape=jax.ShapeDtypeStruct((2 * rows, width), f32),
    )(jnp.reshape(index, (1,)), *(own for own, _ in pairs), *(other for _, other in pairs))


def copy_kernel(source, target):
    target[...] = source[...]


def copied(array, block):
    spec = pl.BlockSpec((block, array.shape[1]), lambda i: (i, 0))
    return pl.pallas_call(
        copy_kernel,
        name="copied",
        grid=(array.shape[0] // block,),
        in_specs=[spec],
        out_specs=spec,
        out_shape=jax.ShapeDtypeStruct(array.shape, array.dtype),
    )(array)


def divide_kernel(where, own, other, weights, places, small):
    heads_half, place_half = weights.shape[0] // 2, places.shape[0] // 2
    top = own.shape[0]

    def fill(low, high):
        weights[:heads_half, :] = low[:heads_half, :]
        weights[heads_half:, :] = high[:heads_half, :]
        places[:place_half, :] = low[heads_half : heads_half + place_half, :]
        places[place_half:, :] = high[heads_half : heads_half + place_half, :]
        small[...] = low[top - 32 :, :]

    @pl.when(where[0] == 0)
    def _():
        fill(own, other)

    @pl.when(where[0] != 0)
    def _():
        fill(other, own)


def mm(first, second):
    return lax.dot_general(first, second, (((1,), (0,)), ((), ())), preferred_element_type=f32)


def mm_nt(first, second):
    return lax.dot_general(first, second, (((1,), (1,)), ((), ())), preferred_element_type=f32)


def mm_tn(first, second):
    return lax.dot_general(first, second, (((0,), (0,)), ((), ())), preferred_element_type=f32)


def normalize(stream):
    centre = stream - jnp.mean(stream, axis=-1, keepdims=True)
    inverse = lax.rsqrt(jnp.mean(centre * centre, axis=-1, keepdims=True) + epsilon)
    return centre * inverse, inverse


def norm_backward(upstream, normed, inverse, gain):
    scaled = upstream * gain
    inner = jnp.mean(scaled * normed, axis=-1, keepdims=True)
    return inverse * (scaled - jnp.mean(scaled, axis=-1, keepdims=True) - normed * inner)


def column_sum(value):
    return jnp.sum(value, axis=0, keepdims=True)


def two_heads(pair, low_lanes):
    zero = jnp.zeros_like(pair)
    return jnp.concatenate(
        [jnp.where(low_lanes, pair, zero), jnp.where(low_lanes, zero, pair)], axis=0
    )


def pair_probs(queries_two, keys_pair, same):
    scores = jnp.where(same, mm_nt(queries_two, keys_pair), big_negative)
    exponent = jnp.exp(scores - jnp.max(scores, axis=-1, keepdims=True))
    return exponent * (1.0 / jnp.sum(exponent, axis=-1, keepdims=True))


def front_kernel(
    tokens,
    place_column,
    sample_column,
    sample_row,
    table,
    one_gain,
    one_shift,
    project_weight,
    joined_bias,
    output_weight,
    output_bias,
    two_gain,
    two_shift,
    stream_out,
    first_out,
    projected_out,
    heads_out,
    mid_out,
    second_out,
):
    rows, width = tokens.shape
    group = sample_row.shape[2]
    scale = (width // HEADS) ** (-0.5)
    places = lax.broadcasted_iota(jnp.int32, (rows, table.shape[0]), 1)
    chosen = (places == place_column[...]).astype(bf16)
    stream = tokens[...].astype(f32) + mm(chosen, table[...])
    stream_out[...] = stream
    normed, _ = normalize(stream)
    first = (normed * one_gain[...] + one_shift[...]).astype(bf16)
    first_out[...] = first
    projected_out[...] = (mm(first, project_weight[...]) + joined_bias[...]).astype(bf16)
    low_lanes = lax.broadcasted_iota(jnp.int32, (group, 128), 1) < 64
    for g in range(rows // group):
        span = slice(g * group, (g + 1) * group)
        same = sample_column[span, :] == sample_row[g]
        same = jnp.concatenate([same, same], axis=0)
        for j in range(width // 128):
            queries = projected_out[span, j * 128 : (j + 1) * 128] * bf16(scale)
            keys = projected_out[span, width + j * 128 : width + (j + 1) * 128]
            values = projected_out[span, 2 * width + j * 128 : 2 * width + (j + 1) * 128]
            probs = pair_probs(two_heads(queries, low_lanes), keys, same)
            both = mm(probs.astype(bf16), values)
            heads_out[span, j * 128 : (j + 1) * 128] = jnp.where(
                low_lanes, both[:group], both[group:]
            ).astype(bf16)
    mid = stream + (mm(heads_out[...], output_weight[...]) + output_bias[...])
    mid_out[...] = mid
    normed, _ = normalize(mid)
    second_out[...] = (normed * two_gain[...] + two_shift[...]).astype(bf16)


def expand_kernel(
    second, cotangent, expand_weight, expand_bias, hidden_out, slope_out, reduce_gradient
):
    before = mm(second[...], expand_weight[...]) + expand_bias[...]
    below = 0.5 * (1.0 + lax.erf(before * (0.5**0.5)))
    density = jnp.exp(-0.5 * before * before) * 0.3989422804014327
    hidden = (before * below).astype(bf16)
    hidden_out[...] = hidden
    slope_out[...] = (below + before * density).astype(bf16)
    reduce_gradient[...] = mm_tn(hidden, cotangent[...])


def reduce_kernel(
    second,
    cotangent,
    before_total,
    before_gradient,
    hidden,
    slope,
    expand_weight,
    reduce_weight,
    reduce_bias,
    total,
    second_gradient,
    expand_gradient,
    bias_gradient,
    *,
    fresh,
):
    step = pl.program_id(0)
    gradient = mm_nt(cotangent[...], reduce_weight[...])
    low = (gradient * slope[...].astype(f32)).astype(bf16)
    bias_gradient[0] = column_sum(low.astype(f32))
    expand_gradient[...] = mm_tn(second[...], low)
    back = mm_nt(low, expand_weight[...])
    ahead = mm(hidden[...], reduce_weight[...])

    @pl.when(step == 0)
    def _():
        if fresh:
            second_gradient[...] = back
            total[...] = before_total[...] + reduce_bias[...] + ahead
        else:
            second_gradient[...] = before_gradient[...] + back
            total[...] = before_total[...] + ahead

    @pl.when(step > 0)
    def _():
        second_gradient[...] += back
        total[...] += ahead


def first_reduce_kernel(
    second, cotangent, mid, hidden, slope, expand_weight, reduce_weight, reduce_bias, *outs
):
    reduce_kernel(
        second, cotangent, mid, None, hidden, slope, expand_weight, reduce_weight, reduce_bias,
        *outs, fresh=True,
    )


def last_reduce_kernel(
    second, cotangent, before_total, before_gradient, hidden, slope, expand_weight,
    reduce_weight, layer_out, second_gradient, expand_gradient, bias_gradient, total,
):
    reduce_kernel(
        second, cotangent, before_total, before_gradient, hidden, slope, expand_weight,
        reduce_weight, None, total, second_gradient, expand_gradient, bias_gradient,
        fresh=False,
    )

    @pl.when(pl.program_id(0) == pl.num_programs(0) - 1)
    def _():
        layer_out[...] = total[...].astype(bf16)


def back_kernel(
    second_gradient,
    mid,
    stream,
    cotangent,
    projected,
    sample_column,
    sample_row,
    one_gain,
    two_gain,
    output_weight,
    project_weight,
    *rest,
):
    token_gradient, in_gradient_out, pieces, branch_out, sums = rest[-5:]
    rows, width = stream.shape
    group = sample_row.shape[2]
    scale = (width // HEADS) ** (-0.5)
    upstream = second_gradient[...]
    out_gradient = cotangent[...].astype(f32)
    normed, inverse = normalize(mid[...])
    two_gain_gradient = column_sum(upstream * normed)
    two_shift_gradient = column_sum(upstream)
    mid_gradient = out_gradient + norm_backward(upstream, normed, inverse, two_gain[...])
    branch = mid_gradient.astype(bf16)
    branch_out[...] = branch
    bias_gradient = column_sum(branch.astype(f32))
    heads_gradient = mm_nt(branch, output_weight[...]).astype(bf16)
    low_lanes = lax.broadcasted_iota(jnp.int32, (group, 128), 1) < 64
    for g in range(rows // group):
        span = slice(g * group, (g + 1) * group)
        same = sample_column[span, :] == sample_row[g]
        same = jnp.concatenate([same, same], axis=0)
        for j in range(width // 128):
            here = [
                slice(k * width + j * 128, k * width + (j + 1) * 128) for k in range(3)
            ]
            queries = two_heads(projected[span, here[0]] * bf16(scale), low_lanes)
            keys = projected[span, here[1]]
            values = projected[span, here[2]]
            upper = two_heads(heads_gradient[span, here[0]], low_lanes)
            probs = pair_probs(queries, keys, same)
            weight_gradient = mm_nt(upper, values)
            inner = jnp.sum(weight_gradient * probs, axis=-1, keepdims=True)
            score_gradient = (probs * (weight_gradient - inner)).astype(bf16)
            both = mm(score_gradient, keys)
            pieces[span, here[0]] = (
                jnp.where(low_lanes, both[:group], both[group:]) * scale
            ).astype(bf16)
            pieces[span, here[1]] = mm_tn(score_gradient, queries).astype(bf16)
            pieces[span, here[2]] = mm_tn(probs.astype(bf16), upper).astype(bf16)
    upstream = mm_nt(pieces[...], project_weight[...])
    normed, inverse = normalize(stream[...])
    in_gradient = mid_gradient + norm_backward(upstream, normed, inverse, one_gain[...])
    in_gradient_out[...] = in_gradient
    token_gradient[...] = in_gradient.astype(bf16)
    sums[0] = jnp.concatenate(
        [
            column_sum(upstream * normed),
            column_sum(upstream),
            column_sum(pieces[:, :width].astype(f32)),
            column_sum(pieces[:, 2 * width :].astype(f32)),
            bias_gradient,
            two_gain_gradient,
            two_shift_gradient,
            column_sum(out_gradient),
        ],
        axis=0,
    )


def project_kernel(first, pieces, project_gradient):
    project_gradient[...] = mm_tn(first[...], pieces[...])


def mixed_kernel(heads, branch, in_gradient, place_row, sums, expand_bias_gradient, mixed):
    rows, width = heads.shape
    top = mixed.shape[0] // 2
    heads_half = width // 2
    place_half = top - heads_half - 32
    both = mm_tn(heads[...], branch[...])
    mixed[:heads_half, :] = both[:heads_half]
    mixed[top : top + heads_half, :] = both[heads_half:]
    high = in_gradient[...].astype(bf16)
    low = (in_gradient[...] - high.astype(f32)).astype(bf16)
    numbers = lax.broadcasted_iota(jnp.int32, (2 * place_half, rows), 0)
    chosen = (numbers == place_row[...]).astype(bf16)
    both = mm(chosen, high) + mm(chosen, low)
    mixed[heads_half : heads_half + place_half, :] = both[:place_half]
    mixed[top + heads_half : top + heads_half + place_half, :] = both[place_half:]
    mixed[top - 32 : top, :] = jnp.zeros((32, width), f32)
    mixed[2 * top - 32 :, :] = jnp.zeros((32, width), f32)
    total = sums[0]
    for k in range(1, sums.shape[0]):
        total = total + sums[k]
    mixed[top - 32 : top - 24, :] = total
    mixed[top - 24 : top - 20, :] = expand_bias_gradient[...]


def whole(array):
    return pl.BlockSpec(array.shape, lambda i: (0,) * array.ndim)


def row_block(array):
    return pl.BlockSpec((BLOCK, array.shape[1]), lambda i: (i, 0))


def lead_block(array, count=1):
    return pl.BlockSpec((count,) + array.shape[1:], lambda i: (i, 0, 0))


def shape(dims, kind):
    return jax.ShapeDtypeStruct(dims, kind)


def body(
    tokens,
    kept_patches,
    resolution,
    position_table,
    norm_one_gain,
    norm_one_shift,
    project_weight,
    query_bias,
    value_bias,
    output_weight,
    output_bias,
    norm_two_gain,
    norm_two_shift,
    expand_weight,
    expand_bias,
    reduce_weight,
    reduce_bias,
    cotangent,
):
    groups, group_rows = kept_patches.shape
    rows, width = tokens.shape
    hidden_width = expand_weight.shape[1]
    places = position_table.shape[0]
    per_step = BLOCK // group_rows
    fine_grid = resolution[:, None] == 1
    place = jnp.where(fine_grid, PATCH_LO + kept_patches, kept_patches % PATCH_LO)
    sample = jnp.where(fine_grid, 0, kept_patches // PATCH_LO)
    place_column = place.reshape(rows, 1)
    place_row = place.reshape(1, rows)
    sample_column = sample.reshape(rows, 1)
    sample_row = sample.reshape(groups, 1, group_rows)

    def line(vector):
        return vector.astype(f32).reshape(1, -1)

    one_gain, two_gain = line(norm_one_gain), line(norm_two_gain)
    joined_bias = line(jnp.concatenate([query_bias, jnp.zeros_like(query_bias), value_bias]))
    front_shapes = (
        shape((rows, width), f32),
        shape((rows, width), bf16),
        shape((rows, 3 * width), bf16),
        shape((rows, width), bf16),
        shape((rows, width), f32),
        shape((rows, width), bf16),
    )
    fixed = (
        position_table,
        one_gain,
        line(norm_one_shift),
        project_weight,
        joined_bias,
        output_weight,
        line(output_bias),
        two_gain,
        line(norm_two_shift),
    )
    stream, first, projected, heads, mid, second = pl.pallas_call(
        front_kernel,
        name="front",
        grid=(rows // BLOCK,),
        in_specs=[
            row_block(tokens),
            row_block(place_column),
            row_block(sample_column),
            lead_block(sample_row, per_step),
        ]
        + [whole(array) for array in fixed],
        out_specs=[row_block(array) for array in front_shapes],
        out_shape=front_shapes,
    )(tokens, place_column, sample_column, sample_row, *fixed)

    columns = pl.BlockSpec((width, WIDE), lambda i: (0, i))
    tall = pl.BlockSpec((rows, WIDE), lambda i: (0, i))
    lines = pl.BlockSpec((WIDE, width), lambda i: (i, 0))
    bias_row = line(expand_bias)
    hidden, slope, reduce_weight_gradient = pl.pallas_call(
        expand_kernel,
        name="expand",
        grid=(hidden_width // WIDE,),
        in_specs=[
            whole(second),
            whole(cotangent),
            columns,
            pl.BlockSpec((1, WIDE), lambda i: (0, i)),
        ],
        out_specs=[tall, tall, lines],
        out_shape=(
            shape((rows, hidden_width), bf16),
            shape((rows, hidden_width), bf16),
            shape((hidden_width, width), f32),
        ),
    )(second, cotangent, expand_weight, bias_row)

    sizes = tuple(lax.axis_size(axis) for axis in AXES)
    paired = sizes == (4, 2, 2, 2)
    order = Order(place_row)
    sums = Sums(sizes, order)
    reduce_weight_gradient, second = order.tie(reduce_weight_gradient, second)
    if paired:
        reduce_weight_gradient = lax.psum_scatter(
            reduce_weight_gradient, CHIPS_FIRST, scatter_dimension=0, tiled=True
        )
    plan = iter(PLAN)

    def advance():
        for name in plan:
            if name == "|":
                break
            if name == "+" and paired:
                sums.results["w"] = lax.all_gather(
                    order.tie(reduce_weight_gradient), CHIPS_FIRST, axis=0, tiled=True
                )
            elif name == "*" and paired:
                sums.results["w"] = order.tie(copied(order.tie(sums.results["w"]), 3 * WIDE // 2))
            elif paired:
                sums.wait(name)
                for both in ("ab", "pq"):
                    if both not in sums.results and all(one in sums.results for one in both):
                        pairs = tuple(order.tie(*sums.results[one]) for one in both)
                        sums.results[both] = order.tie(
                            assemble(lax.axis_index("c"), pairs, 0, width // 2, width // 4)
                        )

    reduce_row = line(reduce_bias)
    half_steps = hidden_width // WIDE // 2
    part = hidden_width // 2
    reduce_shapes = (
        shape((rows, width), f32),
        shape((rows, width), f32),
        shape((width, part), f32),
        shape((half_steps, 1, WIDE), f32),
    )

    def from_step(begin):
        return [
            pl.BlockSpec((rows, WIDE), lambda i: (0, i + begin)),
            pl.BlockSpec((rows, WIDE), lambda i: (0, i + begin)),
            pl.BlockSpec((width, WIDE), lambda i: (0, i + begin)),
            pl.BlockSpec((WIDE, width), lambda i: (i + begin, 0)),
        ]

    reduce_outs = [whole(mid), whole(mid), columns, pl.BlockSpec((1, 1, WIDE), lambda i: (i, 0, 0))]
    so_far, second_gradient, expand_one, bias_one = pl.pallas_call(
        first_reduce_kernel,
        name="reduce_one",
        cost_estimate=SMALL,
        grid=(half_steps,),
        in_specs=[whole(second), whole(cotangent), whole(mid)] + from_step(0) + [whole(reduce_row)],
        out_specs=reduce_outs,
        out_shape=reduce_shapes,
    )(second, cotangent, mid, hidden, slope, expand_weight, reduce_weight, reduce_row)
    if paired:
        sums.begin("a", plane_first([order.tie(expand_one)], sizes))
    advance()
    second_gradient = order.tie(second_gradient)
    layer_output, second_gradient, expand_two, bias_two = pl.pallas_call(
        last_reduce_kernel,
        name="reduce_two",
        cost_estimate=SMALL,
        grid=(half_steps,),
        in_specs=[whole(second), whole(cotangent), whole(mid), whole(mid)] + from_step(half_steps),
        out_specs=[whole(tokens)] + reduce_outs[1:],
        out_shape=(shape((rows, width), bf16),) + reduce_shapes[1:],
        scratch_shapes=[pltpu.VMEM((rows, width), f32)],
    )(second, cotangent, so_far, second_gradient, hidden, slope, expand_weight, reduce_weight)
    expand_two = order.tie(expand_two)
    if paired:
        sums.begin("b", plane_first([expand_two], sizes))
    advance()

    wide_shape = shape((rows, 3 * width), bf16)
    count = rows // BLOCK
    back_shapes = (
        shape((rows, width), bf16),
        shape((rows, width), f32),
        wide_shape,
        shape((rows, width), bf16),
        shape((count, 8, width), f32),
    )
    backs = ()
    for begin in range(count):

        def some(array):
            return pl.BlockSpec((BLOCK, array.shape[1]), lambda i, begin=begin: (begin, 0))

        def lead(size):
            return pl.BlockSpec(size, lambda i, begin=begin: (begin, 0, 0))

        backs = pl.pallas_call(
            back_kernel,
            name="back",
            cost_estimate=SMALL,
            grid=(1,),
            in_specs=[
                some(mid),
                some(mid),
                some(stream),
                some(cotangent),
                some(projected),
                some(sample_column),
                lead((per_step, 1, group_rows)),
                whole(one_gain),
                whole(two_gain),
                whole(output_weight),
                whole(project_weight),
            ]
            + [pl.BlockSpec(memory_space=pl.ANY)] * len(backs),
            out_specs=[some(array) for array in back_shapes[:4]] + [lead((1, 8, width))],
            out_shape=back_shapes,
            input_output_aliases={11 + k: k for k in range(len(backs))},
        )(
            order.tie(second_gradient),
            mid,
            stream,
            cotangent,
            projected,
            sample_column,
            sample_row,
            one_gain,
            two_gain,
            output_weight,
            project_weight,
            *backs,
        )
        backs = order.tie(*backs)
        advance()
    token_gradient, in_gradient, pieces, branch, block_sums = backs

    cut = 3 * width // 2
    narrow_block = width // 2
    project_gradient = pl.pallas_call(
        project_kernel,
        name="project",
        cost_estimate=SMALL,
        grid=(3 * width // narrow_block,),
        in_specs=[whole(first), pl.BlockSpec((rows, narrow_block), lambda i: (0, i))],
        out_specs=pl.BlockSpec((width, narrow_block), lambda i: (0, i)),
        out_shape=shape((width, 3 * width), f32),
    )(first, order.tie(pieces))
    project_gradient = order.tie(project_gradient)
    if paired:
        sums.begin("p", plane_first([project_gradient[:, :cut]], sizes))
        sums.begin("q", plane_first([project_gradient[:, cut:]], sizes))
    advance()
    heads_half, place_half = width // 2, places // 2
    top = heads_half + place_half + 32
    bias_rows = jnp.concatenate([bias_one, bias_two]).reshape(-1, width)
    mixed_inputs = (heads, order.tie(branch), in_gradient, place_row, block_sums, bias_rows)
    mixed_shape = shape((2 * top, width), f32)
    mixed = pl.pallas_call(
        mixed_kernel,
        name="mixed",
        cost_estimate=SMALL,
        grid=(1,),
        in_specs=[whole(array) for array in mixed_inputs],
        out_specs=whole(mixed_shape),
        out_shape=mixed_shape,
    )(*mixed_inputs)
    mixed = order.tie(mixed)
    if paired:
        sums.begin("m", plane_first([mixed], sizes))
        advance()
        core = lax.axis_index("c")
        done = sums.results
        reduce_weight_gradient = done["w"]
        expand_weight_gradient, project_weight_gradient = done["ab"], done["pq"]
        output_weight_gradient, position_gradient, small = pl.pallas_call(
            divide_kernel,
            name="divide",
            in_specs=[pl.BlockSpec(memory_space=pltpu.SMEM)]
            + [pl.BlockSpec(memory_space=pltpu.VMEM)] * 2,
            out_specs=[pl.BlockSpec(memory_space=pltpu.VMEM)] * 3,
            out_shape=(
                shape((width, width), f32),
                shape((places, width), f32),
                shape((32, width), f32),
            ),
        )(jnp.reshape(core, (1,)), *done["m"])
    else:
        (
            reduce_weight_gradient,
            expand_weight_gradient,
            project_weight_gradient,
            mixed,
        ) = lax.psum(
            (
                reduce_weight_gradient,
                jnp.concatenate([expand_one, expand_two], axis=1),
                project_gradient,
                mixed,
            ),
            AXES,
        )
        mixed = mixed.reshape(2, top, width)
        output_weight_gradient = mixed[:, :heads_half].reshape(width, width)
        position_gradient = mixed[:, heads_half : top - 32].reshape(places, width)
        small = mixed[0, top - 32 :]
    (
        norm_one_gain_gradient,
        norm_one_shift_gradient,
        query_bias_gradient,
        value_bias_gradient,
        output_bias_gradient,
        norm_two_gain_gradient,
        norm_two_shift_gradient,
        reduce_bias_gradient,
    ) = (small[k] for k in range(8))
    expand_bias_gradient = small[8:12].reshape(-1)
    return (
        layer_output,
        token_gradient,
        position_gradient,
        norm_one_gain_gradient,
        norm_one_shift_gradient,
        project_weight_gradient,
        query_bias_gradient,
        value_bias_gradient,
        output_weight_gradient,
        output_bias_gradient,
        norm_two_gain_gradient,
        norm_two_shift_gradient,
        expand_weight_gradient,
        expand_bias_gradient,
        reduce_weight_gradient,
        reduce_bias_gradient,
    )


def solution(mesh):
    wide, narrow = mesh.shape["wide"], mesh.shape["narrow"]
    mesh = Mesh(mesh.devices.reshape(wide // 4, 2, 2, narrow), AXES)
    placed = (
        P(AXES, None),
        P(AXES, None),
        P(AXES),
        P(),
        P(),
        P(),
        P(),
        P(),
        P(),
        P(),
        P(),
        P(),
        P(),
        P(),
        P(),
        P(),
        P(),
        P(AXES, None),
    )
    return jax.shard_map(
        body,
        mesh=mesh,
        in_specs=placed,
        out_specs=(
            P(AXES, None),
            P(AXES, None),
            P(),
            P(),
            P(),
            P(),
            P(),
            P(),
            P(),
            P(),
            P(),
            P(),
            P(),
            P(),
            P(),
            P(),
        ),
        check_vma=False,
    )
```

```python
import itertools

import jax
import jax.numpy as jnp
from jax import lax
from jax.experimental import pallas as pl
from jax.experimental.pallas import tpu as pltpu
from jax.sharding import Mesh, PartitionSpec as P

HEADS = 12
PATCH_LO = 128
BLOCK = 256
WIDE = 512
PLAN = "|a|b|a|b|ab||paq+mbpaqbmapqbmpaqb*pmaqpbampqbmpqmpqqmm"

SMALL = pl.CostEstimate(flops=1, transcendentals=0, bytes_accessed=1)

epsilon = 1e-06
big_negative = -1e30
f32 = jnp.float32
bf16 = jnp.bfloat16


AXES = ("z", "y", "c", "x")
CHIPS_FIRST = ("z", "y", "x", "c")


def pairs(sizes, target):
    found = []
    for here in itertools.product(*(range(n) for n in sizes)):
        there = target(*here)
        if there is not None:
            found.append((flat(sizes, here), flat(sizes, there)))
    return found


def flat(sizes, place):
    index = 0
    for n, k in zip(sizes, place):
        index = index * n + k
    return index


def send(value, sizes, target):
    return lax.ppermute(value, AXES, pairs(sizes, target))


def across_core(z, y, c, x):
    return (z, y, 1 - c, x)


def plane_one(z, y, c, x):
    return (z, y, c, 1 - x) if c == 0 else (z, 1 - y, c, x)


def plane_two(z, y, c, x):
    return (z, 1 - y, c, x) if c == 0 else (z, y, c, 1 - x)


def ends_in(z, y, c, x):
    return {0: (1, y, c, x), 3: (2, y, c, x)}.get(z)


def middle(z, y, c, x):
    return {1: (2, y, c, x), 2: (1, y, c, x)}.get(z)


def ends_out(z, y, c, x):
    return {1: (0, y, c, x), 2: (3, y, c, x)}.get(z)


def half(value, index):
    rows = value.shape[0] // 2
    return lax.dynamic_slice_in_dim(value, index * rows, rows, 0)


def join(own, other, index):
    return jnp.concatenate(
        [jnp.where(index == 0, own, other), jnp.where(index == 0, other, own)], axis=0
    )


class Order:
    def __init__(self, token):
        self.token = token

    def tie(self, *values):
        *values, self.token = lax.optimization_barrier((*values, self.token))
        return values[0] if len(values) == 1 else tuple(values)


def plane_first(parts, sizes):
    z, y, c, x = (lax.axis_index(axis) for axis in AXES)
    first = jnp.where(c == 0, x, y)
    second = jnp.where(c == 0, y, x)
    other = sum(half(part, 1 - c) for part in parts)
    came = yield other, across_core
    value = sum(half(part, c) for part in parts) + came
    came = yield half(value, 1 - first), plane_one
    value = half(value, first) + came
    came = yield half(value, 1 - second), plane_two
    value = half(value, second) + came
    value = value + (yield value, ends_in)
    value = value + (yield value, middle)
    came = yield value, ends_out
    value = jnp.where((z == 0) | (z == 3), came, value)
    value = join(value, (yield value, plane_two), second)
    value = join(value, (yield value, plane_one), first)
    came = yield value, across_core
    return value, came


class Sums:
    def __init__(self, sizes, order):
        self.sizes, self.order = sizes, order
        self.steps, self.flying, self.results = {}, {}, {}

    def begin(self, name, steps):
        self.steps[name] = steps
        self.post(name, next(steps))

    def post(self, name, step):
        value, target = step
        if name == "m" and target is across_core and "ab" in self.results:
            value = after(value, self.results["ab"], self.results["w"])
        self.flying[name] = send(self.order.tie(value), self.sizes, target)

    def wait(self, *names):
        for name in names:
            came = self.order.tie(self.flying.pop(name))
            try:
                step = self.steps[name].send(came)
            except StopIteration as stop:
                self.results[name] = stop.value
            else:
                self.post(name, step)


def assemble(index, pairs, begin, rows, block):
    count = len(pairs)
    steps = rows // block
    lead = begin // block
    width = sum(own.shape[1] for own, _ in pairs)

    def kernel(where, *refs):
        mine = pl.program_id(0) == where[0]
        out = refs[-1]
        at = 0
        for own, other in zip(refs[:count], refs[count : 2 * count]):
            span = slice(at, at + own.shape[1])
            at += own.shape[1]

            @pl.when(mine)
            def _():
                out[:, span] = own[...]

            @pl.when(jnp.logical_not(mine))
            def _():
                out[:, span] = other[...]

    def own_map(h, i, where):
        return (lead + jnp.where(h == where[0], i, jnp.where(h == 0, 0, steps - 1)), 0)

    def other_map(h, i, where):
        return (lead + jnp.where(h == where[0], jnp.where(h == 0, 0, steps - 1), i), 0)

    return pl.pallas_call(
        kernel,
        name="assemble",
        grid_spec=pltpu.PrefetchScalarGridSpec(
            num_scalar_prefetch=1,
            grid=(2, steps),
            in_specs=[pl.BlockSpec((block, own.shape[1]), own_map) for own, _ in pairs]
            + [pl.BlockSpec((block, own.shape[1]), other_map) for own, _ in pairs],
            out_specs=pl.BlockSpec((block, width), lambda h, i, where: (h * steps + i, 0)),
        ),
        out_shape=jax.ShapeDtypeStruct((2 * rows, width), f32),
    )(jnp.reshape(index, (1,)), *(own for own, _ in pairs), *(other for _, other in pairs))


def after(value, *others):
    anywhere = pl.BlockSpec(memory_space=pl.ANY)
    return pl.pallas_call(
        lambda *refs: None,
        name="after",
        in_specs=[anywhere] * (1 + len(others)),
        out_specs=anywhere,
        out_shape=jax.ShapeDtypeStruct(value.shape, value.dtype),
        input_output_aliases={0: 0},
    )(value, *others)


def copy_kernel(source, target):
    target[...] = source[...]


def copied(array, block):
    spec = pl.BlockSpec((block, array.shape[1]), lambda i: (i, 0))
    return pl.pallas_call(
        copy_kernel,
        name="copied",
        grid=(array.shape[0] // block,),
        in_specs=[spec],
        out_specs=spec,
        out_shape=jax.ShapeDtypeStruct(array.shape, array.dtype),
    )(array)


def divide_kernel(where, own, other, weights, places, small):
    heads_half, place_half = weights.shape[0] // 2, places.shape[0] // 2
    top = own.shape[0]

    def fill(low, high):
        weights[:heads_half, :] = low[:heads_half, :]
        weights[heads_half:, :] = high[:heads_half, :]
        places[:place_half, :] = low[heads_half : heads_half + place_half, :]
        places[place_half:, :] = high[heads_half : heads_half + place_half, :]
        small[...] = low[top - 32 :, :]

    @pl.when(where[0] == 0)
    def _():
        fill(own, other)

    @pl.when(where[0] != 0)
    def _():
        fill(other, own)


def mm(first, second):
    return lax.dot_general(first, second, (((1,), (0,)), ((), ())), preferred_element_type=f32)


def mm_nt(first, second):
    return lax.dot_general(first, second, (((1,), (1,)), ((), ())), preferred_element_type=f32)


def mm_tn(first, second):
    return lax.dot_general(first, second, (((0,), (0,)), ((), ())), preferred_element_type=f32)


def normalize(stream):
    centre = stream - jnp.mean(stream, axis=-1, keepdims=True)
    inverse = lax.rsqrt(jnp.mean(centre * centre, axis=-1, keepdims=True) + epsilon)
    return centre * inverse, inverse


def norm_backward(upstream, normed, inverse, gain):
    scaled = upstream * gain
    inner = jnp.mean(scaled * normed, axis=-1, keepdims=True)
    return inverse * (scaled - jnp.mean(scaled, axis=-1, keepdims=True) - normed * inner)


def column_sum(value):
    return jnp.sum(value, axis=0, keepdims=True)


def two_heads(pair, low_lanes):
    zero = jnp.zeros_like(pair)
    return jnp.concatenate(
        [jnp.where(low_lanes, pair, zero), jnp.where(low_lanes, zero, pair)], axis=0
    )


def all_probs(queries, keys, same):
    scores = [mm_nt(q, k) for q, k in zip(queries, keys)]
    scores = [jnp.where(same, one, big_negative) for one in scores]
    tops = [jnp.max(one, axis=-1, keepdims=True) for one in scores]
    exponents = [jnp.exp(one - top) for one, top in zip(scores, tops)]
    totals = [jnp.sum(one, axis=-1, keepdims=True) for one in exponents]
    return [one * (1.0 / total) for one, total in zip(exponents, totals)]


def row_of(codes, which):
    return jnp.concatenate([codes[k][which : which + 1] for k in range(codes.shape[0])], axis=1)


def chosen_places(codes, places):
    row = row_of(codes, 0)
    numbers = lax.broadcasted_iota(jnp.int32, (places, row.shape[1]), 0)
    return (numbers == row).astype(bf16)


def same_sample(codes, g):
    numbers = lax.broadcasted_iota(jnp.int32, (16, codes.shape[2]), 0)
    member = (numbers == codes[g][1:2]).astype(bf16)
    same = mm_tn(member, member)
    return jnp.concatenate([same, same], axis=0) > 0.5


def front_kernel(
    tokens,
    codes,
    table,
    lines,
    project_weight,
    output_weight,
    stream_out,
    first_out,
    projected_out,
    heads_out,
    mid_out,
    second_out,
):
    rows, width = tokens.shape
    group = codes.shape[2]
    scale = (width // HEADS) ** (-0.5)
    chosen = chosen_places(codes, table.shape[0])
    stream = tokens[...].astype(f32) + mm_tn(chosen, table[...])
    stream_out[...] = stream
    normed, _ = normalize(stream)
    first = (normed * lines[0:1] + lines[1:2]).astype(bf16)
    first_out[...] = first
    joined_bias = jnp.concatenate([lines[6:7], jnp.zeros((1, width), f32), lines[7:8]], axis=1)
    projected_out[...] = (mm(first, project_weight[...]) + joined_bias).astype(bf16)
    low_lanes = lax.broadcasted_iota(jnp.int32, (group, 128), 1) < 64
    for g in range(rows // group):
        span = slice(g * group, (g + 1) * group)
        same = same_sample(codes, g)
        here = [slice(j * 128, (j + 1) * 128) for j in range(3 * width // 128)]
        count = width // 128
        columns = [projected_out[span, one] for one in here]
        queries = [two_heads(one * bf16(scale), low_lanes) for one in columns[:count]]
        probs = all_probs(queries, columns[count : 2 * count], same)
        both = [mm(p.astype(bf16), v) for p, v in zip(probs, columns[2 * count :])]
        for j in range(count):
            heads_out[span, here[j]] = jnp.where(
                low_lanes, both[j][:group], both[j][group:]
            ).astype(bf16)
    mid = stream + (mm(heads_out[...], output_weight[...]) + lines[4:5])
    mid_out[...] = mid
    normed, _ = normalize(mid)
    second_out[...] = (normed * lines[2:3] + lines[3:4]).astype(bf16)


def expand_kernel(
    second, cotangent, expand_weight, expand_bias, hidden_out, slope_out, reduce_gradient
):
    before = mm(second[...], expand_weight[...]) + expand_bias[...]
    below = 0.5 * (1.0 + lax.erf(before * (0.5**0.5)))
    density = jnp.exp(-0.5 * before * before) * 0.3989422804014327
    hidden = (before * below).astype(bf16)
    hidden_out[...] = hidden
    slope_out[...] = (below + before * density).astype(bf16)
    reduce_gradient[...] = mm_tn(hidden, cotangent[...])


def reduce_kernel(
    second,
    cotangent,
    before_total,
    before_gradient,
    hidden,
    slope,
    expand_weight,
    reduce_weight,
    lines,
    total,
    second_gradient,
    expand_gradient,
    bias_gradient,
    *,
    fresh,
):
    step = pl.program_id(0)
    gradient = mm_nt(cotangent[...], reduce_weight[...])
    low = (gradient * slope[...].astype(f32)).astype(bf16)
    bias_gradient[0] = column_sum(low.astype(f32))
    expand_gradient[...] = mm_tn(second[...], low)
    back = mm_nt(low, expand_weight[...])
    ahead = mm(hidden[...], reduce_weight[...])

    @pl.when(step == 0)
    def _():
        if fresh:
            second_gradient[...] = back
            total[...] = before_total[...] + lines[5:6] + ahead
        else:
            second_gradient[...] = before_gradient[...] + back
            total[...] = before_total[...] + ahead

    @pl.when(step > 0)
    def _():
        second_gradient[...] += back
        total[...] += ahead


def first_reduce_kernel(
    second, cotangent, mid, hidden, slope, expand_weight, reduce_weight, lines, *outs
):
    reduce_kernel(
        second, cotangent, mid, None, hidden, slope, expand_weight, reduce_weight, lines,
        *outs, fresh=True,
    )


def last_reduce_kernel(
    second, cotangent, before_total, before_gradient, hidden, slope, expand_weight,
    reduce_weight, layer_out, second_gradient, expand_gradient, bias_gradient, total,
):
    reduce_kernel(
        second, cotangent, before_total, before_gradient, hidden, slope, expand_weight,
        reduce_weight, None, total, second_gradient, expand_gradient, bias_gradient,
        fresh=False,
    )

    @pl.when(pl.program_id(0) == pl.num_programs(0) - 1)
    def _():
        layer_out[...] = total[...].astype(bf16)


def back_kernel(
    second_gradient,
    mid,
    stream,
    cotangent,
    projected,
    codes,
    lines,
    output_weight,
    project_weight,
    *rest,
):
    token_gradient, in_gradient_out, pieces, branch_out, sums = rest[-5:]
    rows, width = stream.shape
    group = codes.shape[2]
    scale = (width // HEADS) ** (-0.5)
    upstream = second_gradient[...]
    out_gradient = cotangent[...].astype(f32)
    normed, inverse = normalize(mid[...])
    two_gain_gradient = column_sum(upstream * normed)
    two_shift_gradient = column_sum(upstream)
    mid_gradient = out_gradient + norm_backward(upstream, normed, inverse, lines[2:3])
    branch = mid_gradient.astype(bf16)
    branch_out[...] = branch
    bias_gradient = column_sum(branch.astype(f32))
    heads_gradient = mm_nt(branch, output_weight[...]).astype(bf16)
    low_lanes = lax.broadcasted_iota(jnp.int32, (group, 128), 1) < 64
    for g in range(rows // group):
        span = slice(g * group, (g + 1) * group)
        same = same_sample(codes, g)
        here = [slice(j * 128, (j + 1) * 128) for j in range(3 * width // 128)]
        count = width // 128
        columns = [projected[span, one] for one in here]
        queries = [two_heads(one * bf16(scale), low_lanes) for one in columns[:count]]
        keys, values = columns[count : 2 * count], columns[2 * count :]
        uppers = [two_heads(heads_gradient[span, one], low_lanes) for one in here[:count]]
        probs = all_probs(queries, keys, same)
        weights = [mm_nt(upper, v) for upper, v in zip(uppers, values)]
        inner = [jnp.sum(w * p, axis=-1, keepdims=True) for w, p in zip(weights, probs)]
        scores = [(p * (w - n)).astype(bf16) for p, w, n in zip(probs, weights, inner)]
        for_queries = [mm(one, k) for one, k in zip(scores, keys)]
        for_keys = [mm_tn(one, q) for one, q in zip(scores, queries)]
        for_values = [mm_tn(p.astype(bf16), upper) for p, upper in zip(probs, uppers)]
        for j in range(count):
            both = for_queries[j]
            pieces[span, here[j]] = (
                jnp.where(low_lanes, both[:group], both[group:]) * scale
            ).astype(bf16)
            pieces[span, here[count + j]] = for_keys[j].astype(bf16)
            pieces[span, here[2 * count + j]] = for_values[j].astype(bf16)
    upstream = mm_nt(pieces[...], project_weight[...])
    normed, inverse = normalize(stream[...])
    in_gradient = mid_gradient + norm_backward(upstream, normed, inverse, lines[0:1])
    in_gradient_out[...] = in_gradient
    token_gradient[...] = in_gradient.astype(bf16)
    sums[0] = jnp.concatenate(
        [
            column_sum(upstream * normed),
            column_sum(upstream),
            column_sum(pieces[:, :width].astype(f32)),
            column_sum(pieces[:, 2 * width :].astype(f32)),
            bias_gradient,
            two_gain_gradient,
            two_shift_gradient,
            column_sum(out_gradient),
        ],
        axis=0,
    )


def project_kernel(first, pieces, *rest):
    project_gradient = rest[-1]
    project_gradient[...] = mm_tn(first[...], pieces[...])


def mixed_kernel(heads, branch, in_gradient, codes, sums, expand_bias_gradient, *rest):
    mixed = rest[-1]
    width = heads.shape[1]
    top = mixed.shape[0] // 2
    heads_half = width // 2
    place_half = top - heads_half - 32
    both = mm_tn(heads[...], branch[...])
    mixed[:heads_half, :] = both[:heads_half]
    mixed[top : top + heads_half, :] = both[heads_half:]
    high = in_gradient[...].astype(bf16)
    low = (in_gradient[...] - high.astype(f32)).astype(bf16)
    chosen = chosen_places(codes, 2 * place_half)
    both = mm(chosen, high) + mm(chosen, low)
    mixed[heads_half : heads_half + place_half, :] = both[:place_half]
    mixed[top + heads_half : top + heads_half + place_half, :] = both[place_half:]
    mixed[top - 32 : top, :] = jnp.zeros((32, width), f32)
    mixed[2 * top - 32 :, :] = jnp.zeros((32, width), f32)
    total = sums[0]
    for k in range(1, sums.shape[0]):
        total = total + sums[k]
    mixed[top - 32 : top - 24, :] = total
    mixed[top - 24 : top - 20, :] = expand_bias_gradient[...]


def lines_kernel(*refs):
    *vectors, last, lines, bias_row = refs
    for k, vector in enumerate(vectors):
        lines[k : k + 1, :] = vector[...].astype(f32).reshape(1, -1)
    bias_row[...] = last[...].astype(f32).reshape(1, -1)


def whole(array):
    return pl.BlockSpec(array.shape, lambda i: (0,) * array.ndim)


def row_block(array):
    return pl.BlockSpec((BLOCK, array.shape[1]), lambda i: (i, 0))


def lead_block(array, count=1):
    return pl.BlockSpec((count,) + array.shape[1:], lambda i: (i, 0, 0))


def shape(dims, kind):
    return jax.ShapeDtypeStruct(dims, kind)


def body(
    tokens,
    kept_patches,
    resolution,
    position_table,
    norm_one_gain,
    norm_one_shift,
    project_weight,
    query_bias,
    value_bias,
    output_weight,
    output_bias,
    norm_two_gain,
    norm_two_shift,
    expand_weight,
    expand_bias,
    reduce_weight,
    reduce_bias,
    cotangent,
):
    groups, group_rows = kept_patches.shape
    rows, width = tokens.shape
    hidden_width = expand_weight.shape[1]
    places = position_table.shape[0]
    per_step = BLOCK // group_rows
    fine_grid = resolution[:, None] == 1
    place = jnp.where(fine_grid, PATCH_LO + kept_patches, kept_patches % PATCH_LO)
    sample = jnp.where(fine_grid, 0, kept_patches // PATCH_LO)
    codes = jnp.stack([place, sample], axis=1)
    vectors = (
        norm_one_gain,
        norm_one_shift,
        norm_two_gain,
        norm_two_shift,
        output_bias,
        reduce_bias,
        query_bias,
        value_bias,
        expand_bias,
    )
    lines, bias_row = pl.pallas_call(
        lines_kernel,
        name="lines",
        in_specs=[pl.BlockSpec(memory_space=pltpu.VMEM)] * len(vectors),
        out_specs=[pl.BlockSpec(memory_space=pltpu.VMEM)] * 2,
        out_shape=(shape((8, width), f32), shape((1, hidden_width), f32)),
    )(*vectors)
    front_shapes = (
        shape((rows, width), f32),
        shape((rows, width), bf16),
        shape((rows, 3 * width), bf16),
        shape((rows, width), bf16),
        shape((rows, width), f32),
        shape((rows, width), bf16),
    )
    fixed = (position_table, lines, project_weight, output_weight)
    stream, first, projected, heads, mid, second = pl.pallas_call(
        front_kernel,
        name="front",
        grid=(rows // BLOCK,),
        in_specs=[row_block(tokens), lead_block(codes, per_step)]
        + [whole(array) for array in fixed],
        out_specs=[row_block(array) for array in front_shapes],
        out_shape=front_shapes,
    )(tokens, codes, *fixed)

    columns = pl.BlockSpec((width, WIDE), lambda i: (0, i))
    tall = pl.BlockSpec((rows, WIDE), lambda i: (0, i))
    low_lines = pl.BlockSpec((WIDE, width), lambda i: (i, 0))
    hidden, slope, reduce_weight_gradient = pl.pallas_call(
        expand_kernel,
        name="expand",
        grid=(hidden_width // WIDE,),
        in_specs=[
            whole(second),
            whole(cotangent),
            columns,
            pl.BlockSpec((1, WIDE), lambda i: (0, i)),
        ],
        out_specs=[tall, tall, low_lines],
        out_shape=(
            shape((rows, hidden_width), bf16),
            shape((rows, hidden_width), bf16),
            shape((hidden_width, width), f32),
        ),
    )(second, cotangent, expand_weight, bias_row)

    sizes = tuple(lax.axis_size(axis) for axis in AXES)
    paired = sizes == (4, 2, 2, 2)
    order = Order(codes)
    sums = Sums(sizes, order)
    reduce_weight_gradient, second = order.tie(reduce_weight_gradient, second)
    if paired:
        reduce_weight_gradient = lax.psum_scatter(
            reduce_weight_gradient, CHIPS_FIRST, scatter_dimension=0, tiled=True
        )
    plan = iter(PLAN)

    def advance():
        for name in plan:
            if name == "|":
                break
            if name == "+" and paired:
                sums.results["w"] = lax.all_gather(
                    order.tie(reduce_weight_gradient), CHIPS_FIRST, axis=0, tiled=True
                )
            elif name == "*" and paired:
                sums.results["w"] = order.tie(copied(order.tie(sums.results["w"]), 3 * WIDE // 2))
            elif paired:
                sums.wait(name)
                for both in ("ab", "pq"):
                    if both not in sums.results and all(one in sums.results for one in both):
                        pairs = tuple(order.tie(*sums.results[one]) for one in both)
                        sums.results[both] = order.tie(
                            assemble(lax.axis_index("c"), pairs, 0, width // 2, width // 4)
                        )

    half_steps = hidden_width // WIDE // 2
    part = hidden_width // 2
    reduce_shapes = (
        shape((rows, width), f32),
        shape((rows, width), f32),
        shape((width, part), f32),
        shape((half_steps, 1, WIDE), f32),
    )

    def from_step(begin):
        return [
            pl.BlockSpec((rows, WIDE), lambda i: (0, i + begin)),
            pl.BlockSpec((rows, WIDE), lambda i: (0, i + begin)),
            pl.BlockSpec((width, WIDE), lambda i: (0, i + begin)),
            pl.BlockSpec((WIDE, width), lambda i: (i + begin, 0)),
        ]

    reduce_outs = [whole(mid), whole(mid), columns, pl.BlockSpec((1, 1, WIDE), lambda i: (i, 0, 0))]
    so_far, second_gradient, expand_one, bias_one = pl.pallas_call(
        first_reduce_kernel,
        name="reduce_one",
        cost_estimate=SMALL,
        grid=(half_steps,),
        in_specs=[whole(second), whole(cotangent), whole(mid)] + from_step(0) + [whole(lines)],
        out_specs=reduce_outs,
        out_shape=reduce_shapes,
    )(second, cotangent, mid, hidden, slope, expand_weight, reduce_weight, lines)
    if paired:
        sums.begin("a", plane_first([order.tie(expand_one)], sizes))
    advance()
    second_gradient = order.tie(second_gradient)
    layer_output, second_gradient, expand_two, bias_two = pl.pallas_call(
        last_reduce_kernel,
        name="reduce_two",
        cost_estimate=SMALL,
        grid=(half_steps,),
        in_specs=[whole(second), whole(cotangent), whole(mid), whole(mid)] + from_step(half_steps),
        out_specs=[whole(tokens)] + reduce_outs[1:],
        out_shape=(shape((rows, width), bf16),) + reduce_shapes[1:],
        scratch_shapes=[pltpu.VMEM((rows, width), f32)],
    )(second, cotangent, so_far, second_gradient, hidden, slope, expand_weight, reduce_weight)
    expand_two = order.tie(expand_two)
    if paired:
        sums.begin("b", plane_first([expand_two], sizes))
    advance()

    wide_shape = shape((rows, 3 * width), bf16)
    count = rows // BLOCK
    back_shapes = (
        shape((rows, width), bf16),
        shape((rows, width), f32),
        wide_shape,
        shape((rows, width), bf16),
        shape((count, 8, width), f32),
    )
    backs = ()
    for begin in range(count):

        def some(array):
            return pl.BlockSpec((BLOCK, array.shape[1]), lambda i, begin=begin: (begin, 0))

        def lead(size):
            return pl.BlockSpec(size, lambda i, begin=begin: (begin, 0, 0))

        backs = pl.pallas_call(
            back_kernel,
            name="back",
            cost_estimate=SMALL,
            grid=(1,),
            in_specs=[
                some(mid),
                some(mid),
                some(stream),
                some(cotangent),
                some(projected),
                lead((per_step,) + codes.shape[1:]),
                whole(lines),
                whole(output_weight),
                whole(project_weight),
            ]
            + [pl.BlockSpec(memory_space=pl.ANY)] * len(backs),
            out_specs=[some(array) for array in back_shapes[:4]] + [lead((1, 8, width))],
            out_shape=back_shapes,
            input_output_aliases={9 + k: k for k in range(len(backs))},
        )(
            order.tie(second_gradient),
            mid,
            stream,
            cotangent,
            projected,
            codes,
            lines,
            output_weight,
            project_weight,
            *backs,
        )
        backs = order.tie(*backs)
        advance()
    token_gradient, in_gradient, pieces, branch, block_sums = backs

    cut = 3 * width // 2
    narrow_block = width // 2
    project_gradient = pl.pallas_call(
        project_kernel,
        name="project",
        cost_estimate=SMALL,
        grid=(3 * width // narrow_block,),
        in_specs=[whole(first), pl.BlockSpec((rows, narrow_block), lambda i: (0, i))],
        out_specs=pl.BlockSpec((width, narrow_block), lambda i: (0, i)),
        out_shape=shape((width, 3 * width), f32),
    )(first, order.tie(pieces))
    project_gradient = order.tie(project_gradient)
    if paired:
        sums.begin("p", plane_first([project_gradient[:, :cut]], sizes))
        sums.begin("q", plane_first([project_gradient[:, cut:]], sizes))
    advance()
    heads_half, place_half = width // 2, places // 2
    top = heads_half + place_half + 32
    bias_rows = jnp.concatenate([bias_one, bias_two]).reshape(-1, width)
    mixed_inputs = (heads, order.tie(branch), in_gradient, codes, block_sums, bias_rows)
    mixed_shape = shape((2 * top, width), f32)
    mixed = pl.pallas_call(
        mixed_kernel,
        name="mixed",
        cost_estimate=SMALL,
        grid=(1,),
        in_specs=[whole(array) for array in mixed_inputs],
        out_specs=whole(mixed_shape),
        out_shape=mixed_shape,
    )(*mixed_inputs)
    mixed = order.tie(mixed)
    if paired:
        sums.begin("m", plane_first([mixed], sizes))
        advance()
        core = lax.axis_index("c")
        done = sums.results
        reduce_weight_gradient = done["w"]
        expand_weight_gradient, project_weight_gradient = done["ab"], done["pq"]
        output_weight_gradient, position_gradient, small = pl.pallas_call(
            divide_kernel,
            name="divide",
            in_specs=[pl.BlockSpec(memory_space=pltpu.SMEM)]
            + [pl.BlockSpec(memory_space=pltpu.VMEM)] * 2,
            out_specs=[pl.BlockSpec(memory_space=pltpu.VMEM)] * 3,
            out_shape=(
                shape((width, width), f32),
                shape((places, width), f32),
                shape((32, width), f32),
            ),
        )(jnp.reshape(core, (1,)), *done["m"])
    else:
        (
            reduce_weight_gradient,
            expand_weight_gradient,
            project_weight_gradient,
            mixed,
        ) = lax.psum(
            (
                reduce_weight_gradient,
                jnp.concatenate([expand_one, expand_two], axis=1),
                project_gradient,
                mixed,
            ),
            AXES,
        )
        mixed = mixed.reshape(2, top, width)
        output_weight_gradient = mixed[:, :heads_half].reshape(width, width)
        position_gradient = mixed[:, heads_half : top - 32].reshape(places, width)
        small = mixed[0, top - 32 :]
    (
        norm_one_gain_gradient,
        norm_one_shift_gradient,
        query_bias_gradient,
        value_bias_gradient,
        output_bias_gradient,
        norm_two_gain_gradient,
        norm_two_shift_gradient,
        reduce_bias_gradient,
    ) = (small[k] for k in range(8))
    expand_bias_gradient = small[8:12].reshape(-1)
    return (
        layer_output,
        token_gradient,
        position_gradient,
        norm_one_gain_gradient,
        norm_one_shift_gradient,
        project_weight_gradient,
        query_bias_gradient,
        value_bias_gradient,
        output_weight_gradient,
        output_bias_gradient,
        norm_two_gain_gradient,
        norm_two_shift_gradient,
        expand_weight_gradient,
        expand_bias_gradient,
        reduce_weight_gradient,
        reduce_bias_gradient,
    )


def solution(mesh):
    wide, narrow = mesh.shape["wide"], mesh.shape["narrow"]
    mesh = Mesh(mesh.devices.reshape(wide // 4, 2, 2, narrow), AXES)
    placed = (
        P(AXES, None),
        P(AXES, None),
        P(AXES),
        P(),
        P(),
        P(),
        P(),
        P(),
        P(),
        P(),
        P(),
        P(),
        P(),
        P(),
        P(),
        P(),
        P(),
        P(AXES, None),
    )
    return jax.shard_map(
        body,
        mesh=mesh,
        in_specs=placed,
        out_specs=(
            P(AXES, None),
            P(AXES, None),
            P(),
            P(),
            P(),
            P(),
            P(),
            P(),
            P(),
            P(),
            P(),
            P(),
            P(),
            P(),
            P(),
            P(),
        ),
        check_vma=False,
    )
```

```python
import itertools

import jax
import jax.numpy as jnp
from jax import lax
from jax.experimental import pallas as pl
from jax.experimental.pallas import tpu as pltpu
from jax.sharding import Mesh, PartitionSpec as P

HEADS = 12
PATCH_LO = 128
BLOCK = 256
WIDE = 512
PLAN = "|a|b|a|b|ab||paq+mbpaqbmapqbmpaqb*pmaqpbampqbmpqmpqqmm"

SMALL = pl.CostEstimate(flops=1, transcendentals=0, bytes_accessed=1)

epsilon = 1e-06
big_negative = -1e30
f32 = jnp.float32
bf16 = jnp.bfloat16


AXES = ("z", "y", "c", "x")
CHIPS_FIRST = ("z", "y", "x", "c")


def pairs(sizes, target):
    found = []
    for here in itertools.product(*(range(n) for n in sizes)):
        there = target(*here)
        if there is not None:
            found.append((flat(sizes, here), flat(sizes, there)))
    return found


def flat(sizes, place):
    index = 0
    for n, k in zip(sizes, place):
        index = index * n + k
    return index


def send(value, sizes, target):
    return lax.ppermute(value, AXES, pairs(sizes, target))


def across_core(z, y, c, x):
    return (z, y, 1 - c, x)


def plane_one(z, y, c, x):
    return (z, y, c, 1 - x) if c == 0 else (z, 1 - y, c, x)


def plane_two(z, y, c, x):
    return (z, 1 - y, c, x) if c == 0 else (z, y, c, 1 - x)


def ends_in(z, y, c, x):
    return {0: (1, y, c, x), 3: (2, y, c, x)}.get(z)


def middle(z, y, c, x):
    return {1: (2, y, c, x), 2: (1, y, c, x)}.get(z)


def ends_out(z, y, c, x):
    return {1: (0, y, c, x), 2: (3, y, c, x)}.get(z)


def half(value, index):
    rows = value.shape[0] // 2
    return lax.dynamic_slice_in_dim(value, index * rows, rows, 0)


def join(own, other, index):
    return jnp.concatenate(
        [jnp.where(index == 0, own, other), jnp.where(index == 0, other, own)], axis=0
    )


class Order:
    def __init__(self, token):
        self.token = token

    def tie(self, *values):
        *values, self.token = lax.optimization_barrier((*values, self.token))
        return values[0] if len(values) == 1 else tuple(values)


def plane_first(parts, sizes):
    z, y, c, x = (lax.axis_index(axis) for axis in AXES)
    first = jnp.where(c == 0, x, y)
    second = jnp.where(c == 0, y, x)
    other = sum(half(part, 1 - c) for part in parts)
    came = yield other, across_core
    value = sum(half(part, c) for part in parts) + came
    came = yield half(value, 1 - first), plane_one
    value = half(value, first) + came
    came = yield half(value, 1 - second), plane_two
    value = half(value, second) + came
    value = value + (yield value, ends_in)
    value = value + (yield value, middle)
    came = yield value, ends_out
    value = jnp.where((z == 0) | (z == 3), came, value)
    value = join(value, (yield value, plane_two), second)
    value = join(value, (yield value, plane_one), first)
    came = yield value, across_core
    return value, came


class Sums:
    def __init__(self, sizes, order):
        self.sizes, self.order = sizes, order
        self.steps, self.flying, self.results = {}, {}, {}

    def begin(self, name, steps):
        self.steps[name] = steps
        self.post(name, next(steps))

    def post(self, name, step):
        value, target = step
        if name == "m" and target is across_core and "ab" in self.results:
            value = after(value, self.results["ab"], self.results["w"])
        self.flying[name] = send(self.order.tie(value), self.sizes, target)

    def wait(self, *names):
        for name in names:
            came = self.order.tie(self.flying.pop(name))
            try:
                step = self.steps[name].send(came)
            except StopIteration as stop:
                self.results[name] = stop.value
            else:
                self.post(name, step)


def assemble(index, pairs, begin, rows, block):
    count = len(pairs)
    steps = rows // block
    lead = begin // block
    width = sum(own.shape[1] for own, _ in pairs)

    def kernel(where, *refs):
        mine = pl.program_id(0) == where[0]
        out = refs[-1]
        at = 0
        for own, other in zip(refs[:count], refs[count : 2 * count]):
            span = slice(at, at + own.shape[1])
            at += own.shape[1]

            @pl.when(mine)
            def _():
                out[:, span] = own[...]

            @pl.when(jnp.logical_not(mine))
            def _():
                out[:, span] = other[...]

    def own_map(h, i, where):
        return (lead + jnp.where(h == where[0], i, jnp.where(h == 0, 0, steps - 1)), 0)

    def other_map(h, i, where):
        return (lead + jnp.where(h == where[0], jnp.where(h == 0, 0, steps - 1), i), 0)

    return pl.pallas_call(
        kernel,
        name="assemble",
        grid_spec=pltpu.PrefetchScalarGridSpec(
            num_scalar_prefetch=1,
            grid=(2, steps),
            in_specs=[pl.BlockSpec((block, own.shape[1]), own_map) for own, _ in pairs]
            + [pl.BlockSpec((block, own.shape[1]), other_map) for own, _ in pairs],
            out_specs=pl.BlockSpec((block, width), lambda h, i, where: (h * steps + i, 0)),
        ),
        out_shape=jax.ShapeDtypeStruct((2 * rows, width), f32),
    )(jnp.reshape(index, (1,)), *(own for own, _ in pairs), *(other for _, other in pairs))


def after(value, *others):
    anywhere = pl.BlockSpec(memory_space=pl.ANY)
    return pl.pallas_call(
        lambda *refs: None,
        name="after",
        in_specs=[anywhere] * (1 + len(others)),
        out_specs=anywhere,
        out_shape=jax.ShapeDtypeStruct(value.shape, value.dtype),
        input_output_aliases={0: 0},
    )(value, *others)


def copy_kernel(source, target):
    target[...] = source[...]


def copied(array, block):
    spec = pl.BlockSpec((block, array.shape[1]), lambda i: (i, 0))
    return pl.pallas_call(
        copy_kernel,
        name="copied",
        grid=(array.shape[0] // block,),
        in_specs=[spec],
        out_specs=spec,
        out_shape=jax.ShapeDtypeStruct(array.shape, array.dtype),
    )(array)


def divide_kernel(where, own, other, weights, places, small):
    heads_half, place_half = weights.shape[0] // 2, places.shape[0] // 2
    top = own.shape[0]

    def fill(low, high):
        weights[:heads_half, :] = low[:heads_half, :]
        weights[heads_half:, :] = high[:heads_half, :]
        places[:place_half, :] = low[heads_half : heads_half + place_half, :]
        places[place_half:, :] = high[heads_half : heads_half + place_half, :]
        small[...] = low[top - 32 :, :]

    @pl.when(where[0] == 0)
    def _():
        fill(own, other)

    @pl.when(where[0] != 0)
    def _():
        fill(other, own)


def mm(first, second):
    return lax.dot_general(first, second, (((1,), (0,)), ((), ())), preferred_element_type=f32)


def mm_nt(first, second):
    return lax.dot_general(first, second, (((1,), (1,)), ((), ())), preferred_element_type=f32)


def mm_tn(first, second):
    return lax.dot_general(first, second, (((0,), (0,)), ((), ())), preferred_element_type=f32)


def normalize(stream):
    centre = stream - jnp.mean(stream, axis=-1, keepdims=True)
    inverse = lax.rsqrt(jnp.mean(centre * centre, axis=-1, keepdims=True) + epsilon)
    return centre * inverse, inverse


def norm_backward(upstream, normed, inverse, gain):
    scaled = upstream * gain
    inner = jnp.mean(scaled * normed, axis=-1, keepdims=True)
    return inverse * (scaled - jnp.mean(scaled, axis=-1, keepdims=True) - normed * inner)


def column_sum(value):
    return jnp.sum(value, axis=0, keepdims=True)


def two_heads(pair, low_lanes):
    zero = jnp.zeros_like(pair)
    return jnp.concatenate(
        [jnp.where(low_lanes, pair, zero), jnp.where(low_lanes, zero, pair)], axis=0
    )


def all_probs(queries, keys, same):
    scores = [mm_nt(q, k) for q, k in zip(queries, keys)]
    scores = [jnp.where(same, one, big_negative) for one in scores]
    tops = [jnp.max(one, axis=-1, keepdims=True) for one in scores]
    exponents = [jnp.exp(one - top) for one, top in zip(scores, tops)]
    totals = [jnp.sum(one, axis=-1, keepdims=True) for one in exponents]
    return [one * (1.0 / total) for one, total in zip(exponents, totals)]


def row_of(codes, which):
    return jnp.concatenate([codes[k][which : which + 1] for k in range(codes.shape[0])], axis=1)


def chosen_places(codes, places):
    row = row_of(codes, 0)
    numbers = lax.broadcasted_iota(jnp.int32, (places, row.shape[1]), 0)
    return (numbers == row).astype(bf16)


def same_sample(codes, g):
    numbers = lax.broadcasted_iota(jnp.int32, (16, codes.shape[2]), 0)
    member = (numbers == codes[g][1:2]).astype(bf16)
    same = mm_tn(member, member)
    return jnp.concatenate([same, same], axis=0) > 0.5


def front_kernel(
    tokens,
    codes,
    table,
    lines,
    project_weight,
    output_weight,
    stream_out,
    first_out,
    projected_out,
    heads_out,
    mid_out,
    second_out,
):
    rows, width = tokens.shape
    group = codes.shape[2]
    scale = (width // HEADS) ** (-0.5)
    chosen = chosen_places(codes, table.shape[0])
    stream = tokens[...].astype(f32) + mm_tn(chosen, table[...])
    stream_out[...] = stream
    normed, _ = normalize(stream)
    first = (normed * lines[0:1] + lines[1:2]).astype(bf16)
    first_out[...] = first
    joined_bias = jnp.concatenate([lines[6:7], jnp.zeros((1, width), f32), lines[7:8]], axis=1)
    projected_out[...] = (mm(first, project_weight[...]) + joined_bias).astype(bf16)
    low_lanes = lax.broadcasted_iota(jnp.int32, (group, 128), 1) < 64
    def one_group(g, carry):
        span = pl.ds(pl.multiple_of(g * group, group), group)
        same = same_sample(codes, g)
        here = [slice(j * 128, (j + 1) * 128) for j in range(3 * width // 128)]
        count = width // 128
        columns = [projected_out[span, one] for one in here]
        queries = [two_heads(one * bf16(scale), low_lanes) for one in columns[:count]]
        probs = all_probs(queries, columns[count : 2 * count], same)
        both = [mm(p.astype(bf16), v) for p, v in zip(probs, columns[2 * count :])]
        for j in range(count):
            heads_out[span, here[j]] = jnp.where(
                low_lanes, both[j][:group], both[j][group:]
            ).astype(bf16)
        return carry

    lax.fori_loop(0, rows // group, one_group, 0)
    mid = stream + (mm(heads_out[...], output_weight[...]) + lines[4:5])
    mid_out[...] = mid
    normed, _ = normalize(mid)
    second_out[...] = (normed * lines[2:3] + lines[3:4]).astype(bf16)


def expand_kernel(
    second, cotangent, expand_weight, expand_bias, hidden_out, slope_out, reduce_gradient
):
    before = mm(second[...], expand_weight[...]) + expand_bias[...]
    below = 0.5 * (1.0 + lax.erf(before * (0.5**0.5)))
    density = jnp.exp(-0.5 * before * before) * 0.3989422804014327
    hidden = (before * below).astype(bf16)
    hidden_out[...] = hidden
    slope_out[...] = (below + before * density).astype(bf16)
    reduce_gradient[...] = mm_tn(hidden, cotangent[...])


def reduce_kernel(
    second,
    cotangent,
    before_total,
    before_gradient,
    hidden,
    slope,
    expand_weight,
    reduce_weight,
    lines,
    total,
    second_gradient,
    expand_gradient,
    bias_gradient,
    *,
    fresh,
):
    step = pl.program_id(0)
    gradient = mm_nt(cotangent[...], reduce_weight[...])
    low = (gradient * slope[...].astype(f32)).astype(bf16)
    bias_gradient[0] = column_sum(low.astype(f32))
    expand_gradient[...] = mm_tn(second[...], low)
    back = mm_nt(low, expand_weight[...])
    ahead = mm(hidden[...], reduce_weight[...])

    @pl.when(step == 0)
    def _():
        if fresh:
            second_gradient[...] = back
            total[...] = before_total[...] + lines[5:6] + ahead
        else:
            second_gradient[...] = before_gradient[...] + back
            total[...] = before_total[...] + ahead

    @pl.when(step > 0)
    def _():
        second_gradient[...] += back
        total[...] += ahead


def first_reduce_kernel(
    second, cotangent, mid, hidden, slope, expand_weight, reduce_weight, lines, *outs
):
    reduce_kernel(
        second, cotangent, mid, None, hidden, slope, expand_weight, reduce_weight, lines,
        *outs, fresh=True,
    )


def last_reduce_kernel(
    second, cotangent, before_total, before_gradient, hidden, slope, expand_weight,
    reduce_weight, layer_out, second_gradient, expand_gradient, bias_gradient, total,
):
    reduce_kernel(
        second, cotangent, before_total, before_gradient, hidden, slope, expand_weight,
        reduce_weight, None, total, second_gradient, expand_gradient, bias_gradient,
        fresh=False,
    )

    @pl.when(pl.program_id(0) == pl.num_programs(0) - 1)
    def _():
        layer_out[...] = total[...].astype(bf16)


def back_kernel(
    second_gradient,
    mid,
    stream,
    cotangent,
    projected,
    codes,
    lines,
    output_weight,
    project_weight,
    *rest,
):
    token_gradient, in_gradient_out, pieces, branch_out, sums = rest[-5:]
    rows, width = stream.shape
    group = codes.shape[2]
    scale = (width // HEADS) ** (-0.5)
    upstream = second_gradient[...]
    out_gradient = cotangent[...].astype(f32)
    normed, inverse = normalize(mid[...])
    two_gain_gradient = column_sum(upstream * normed)
    two_shift_gradient = column_sum(upstream)
    mid_gradient = out_gradient + norm_backward(upstream, normed, inverse, lines[2:3])
    branch = mid_gradient.astype(bf16)
    branch_out[...] = branch
    bias_gradient = column_sum(branch.astype(f32))
    heads_gradient = mm_nt(branch, output_weight[...]).astype(bf16)
    low_lanes = lax.broadcasted_iota(jnp.int32, (group, 128), 1) < 64
    token_gradient[...] = heads_gradient

    def one_group(g, carry):
        span = pl.ds(pl.multiple_of(g * group, group), group)
        same = same_sample(codes, g)
        here = [slice(j * 128, (j + 1) * 128) for j in range(3 * width // 128)]
        count = width // 128
        columns = [projected[span, one] for one in here]
        queries = [two_heads(one * bf16(scale), low_lanes) for one in columns[:count]]
        keys, values = columns[count : 2 * count], columns[2 * count :]
        uppers = [two_heads(token_gradient[span, one], low_lanes) for one in here[:count]]
        probs = all_probs(queries, keys, same)
        weights = [mm_nt(upper, v) for upper, v in zip(uppers, values)]
        inner = [jnp.sum(w * p, axis=-1, keepdims=True) for w, p in zip(weights, probs)]
        scores = [(p * (w - n)).astype(bf16) for p, w, n in zip(probs, weights, inner)]
        for_queries = [mm(one, k) for one, k in zip(scores, keys)]
        for_keys = [mm_tn(one, q) for one, q in zip(scores, queries)]
        for_values = [mm_tn(p.astype(bf16), upper) for p, upper in zip(probs, uppers)]
        for j in range(count):
            both = for_queries[j]
            pieces[span, here[j]] = (
                jnp.where(low_lanes, both[:group], both[group:]) * scale
            ).astype(bf16)
            pieces[span, here[count + j]] = for_keys[j].astype(bf16)
            pieces[span, here[2 * count + j]] = for_values[j].astype(bf16)
        return carry

    lax.fori_loop(0, rows // group, one_group, 0)
    upstream = mm_nt(pieces[...], project_weight[...])
    normed, inverse = normalize(stream[...])
    in_gradient = mid_gradient + norm_backward(upstream, normed, inverse, lines[0:1])
    in_gradient_out[...] = in_gradient
    token_gradient[...] = in_gradient.astype(bf16)
    sums[0] = jnp.concatenate(
        [
            column_sum(upstream * normed),
            column_sum(upstream),
            column_sum(pieces[:, :width].astype(f32)),
            column_sum(pieces[:, 2 * width :].astype(f32)),
            bias_gradient,
            two_gain_gradient,
            two_shift_gradient,
            column_sum(out_gradient),
        ],
        axis=0,
    )


def project_kernel(first, pieces, *rest):
    project_gradient = rest[-1]
    project_gradient[...] = mm_tn(first[...], pieces[...])


def mixed_kernel(heads, branch, in_gradient, codes, sums, expand_bias_gradient, *rest):
    mixed = rest[-1]
    width = heads.shape[1]
    top = mixed.shape[0] // 2
    heads_half = width // 2
    place_half = top - heads_half - 32
    both = mm_tn(heads[...], branch[...])
    mixed[:heads_half, :] = both[:heads_half]
    mixed[top : top + heads_half, :] = both[heads_half:]
    high = in_gradient[...].astype(bf16)
    low = (in_gradient[...] - high.astype(f32)).astype(bf16)
    chosen = chosen_places(codes, 2 * place_half)
    both = mm(chosen, high) + mm(chosen, low)
    mixed[heads_half : heads_half + place_half, :] = both[:place_half]
    mixed[top + heads_half : top + heads_half + place_half, :] = both[place_half:]
    mixed[top - 32 : top, :] = jnp.zeros((32, width), f32)
    mixed[2 * top - 32 :, :] = jnp.zeros((32, width), f32)
    total = sums[0]
    for k in range(1, sums.shape[0]):
        total = total + sums[k]
    mixed[top - 32 : top - 24, :] = total
    mixed[top - 24 : top - 20, :] = expand_bias_gradient[...]


def lines_kernel(*refs):
    *vectors, last, lines, bias_row = refs
    for k, vector in enumerate(vectors):
        lines[k : k + 1, :] = vector[...].astype(f32).reshape(1, -1)
    bias_row[...] = last[...].astype(f32).reshape(1, -1)


def whole(array):
    return pl.BlockSpec(array.shape, lambda i: (0,) * array.ndim)


def row_block(array):
    return pl.BlockSpec((BLOCK, array.shape[1]), lambda i: (i, 0))


def lead_block(array, count=1):
    return pl.BlockSpec((count,) + array.shape[1:], lambda i: (i, 0, 0))


def shape(dims, kind):
    return jax.ShapeDtypeStruct(dims, kind)


def body(
    tokens,
    kept_patches,
    resolution,
    position_table,
    norm_one_gain,
    norm_one_shift,
    project_weight,
    query_bias,
    value_bias,
    output_weight,
    output_bias,
    norm_two_gain,
    norm_two_shift,
    expand_weight,
    expand_bias,
    reduce_weight,
    reduce_bias,
    cotangent,
):
    groups, group_rows = kept_patches.shape
    rows, width = tokens.shape
    hidden_width = expand_weight.shape[1]
    places = position_table.shape[0]
    per_step = BLOCK // group_rows
    fine_grid = resolution[:, None] == 1
    place = jnp.where(fine_grid, PATCH_LO + kept_patches, kept_patches % PATCH_LO)
    sample = jnp.where(fine_grid, 0, kept_patches // PATCH_LO)
    codes = jnp.stack([place, sample], axis=1)
    vectors = (
        norm_one_gain,
        norm_one_shift,
        norm_two_gain,
        norm_two_shift,
        output_bias,
        reduce_bias,
        query_bias,
        value_bias,
        expand_bias,
    )
    lines, bias_row = pl.pallas_call(
        lines_kernel,
        name="lines",
        in_specs=[pl.BlockSpec(memory_space=pltpu.VMEM)] * len(vectors),
        out_specs=[pl.BlockSpec(memory_space=pltpu.VMEM)] * 2,
        out_shape=(shape((8, width), f32), shape((1, hidden_width), f32)),
    )(*vectors)
    front_shapes = (
        shape((rows, width), f32),
        shape((rows, width), bf16),
        shape((rows, 3 * width), bf16),
        shape((rows, width), bf16),
        shape((rows, width), f32),
        shape((rows, width), bf16),
    )
    fixed = (position_table, lines, project_weight, output_weight)
    stream, first, projected, heads, mid, second = pl.pallas_call(
        front_kernel,
        name="front",
        grid=(rows // BLOCK,),
        in_specs=[row_block(tokens), lead_block(codes, per_step)]
        + [whole(array) for array in fixed],
        out_specs=[row_block(array) for array in front_shapes],
        out_shape=front_shapes,
    )(tokens, codes, *fixed)

    columns = pl.BlockSpec((width, WIDE), lambda i: (0, i))
    tall = pl.BlockSpec((rows, WIDE), lambda i: (0, i))
    low_lines = pl.BlockSpec((WIDE, width), lambda i: (i, 0))
    hidden, slope, reduce_weight_gradient = pl.pallas_call(
        expand_kernel,
        name="expand",
        grid=(hidden_width // WIDE,),
        in_specs=[
            whole(second),
            whole(cotangent),
            columns,
            pl.BlockSpec((1, WIDE), lambda i: (0, i)),
        ],
        out_specs=[tall, tall, low_lines],
        out_shape=(
            shape((rows, hidden_width), bf16),
            shape((rows, hidden_width), bf16),
            shape((hidden_width, width), f32),
        ),
    )(second, cotangent, expand_weight, bias_row)

    sizes = tuple(lax.axis_size(axis) for axis in AXES)
    paired = sizes == (4, 2, 2, 2)
    order = Order(codes)
    sums = Sums(sizes, order)
    reduce_weight_gradient, second = order.tie(reduce_weight_gradient, second)
    if paired:
        reduce_weight_gradient = lax.psum_scatter(
            reduce_weight_gradient, CHIPS_FIRST, scatter_dimension=0, tiled=True
        )
    plan = iter(PLAN)

    def advance():
        for name in plan:
            if name == "|":
                break
            if name == "+" and paired:
                sums.results["w"] = lax.all_gather(
                    order.tie(reduce_weight_gradient), CHIPS_FIRST, axis=0, tiled=True
                )
            elif name == "*" and paired:
                sums.results["w"] = order.tie(copied(order.tie(sums.results["w"]), 3 * WIDE // 2))
            elif paired:
                sums.wait(name)
                for both in ("ab", "pq"):
                    if both not in sums.results and all(one in sums.results for one in both):
                        pairs = tuple(order.tie(*sums.results[one]) for one in both)
                        sums.results[both] = order.tie(
                            assemble(lax.axis_index("c"), pairs, 0, width // 2, width // 4)
                        )

    half_steps = hidden_width // WIDE // 2
    part = hidden_width // 2
    reduce_shapes = (
        shape((rows, width), f32),
        shape((rows, width), f32),
        shape((width, part), f32),
        shape((half_steps, 1, WIDE), f32),
    )

    def from_step(begin):
        return [
            pl.BlockSpec((rows, WIDE), lambda i: (0, i + begin)),
            pl.BlockSpec((rows, WIDE), lambda i: (0, i + begin)),
            pl.BlockSpec((width, WIDE), lambda i: (0, i + begin)),
            pl.BlockSpec((WIDE, width), lambda i: (i + begin, 0)),
        ]

    reduce_outs = [whole(mid), whole(mid), columns, pl.BlockSpec((1, 1, WIDE), lambda i: (i, 0, 0))]
    so_far, second_gradient, expand_one, bias_one = pl.pallas_call(
        first_reduce_kernel,
        name="reduce_one",
        cost_estimate=SMALL,
        grid=(half_steps,),
        in_specs=[whole(second), whole(cotangent), whole(mid)] + from_step(0) + [whole(lines)],
        out_specs=reduce_outs,
        out_shape=reduce_shapes,
    )(second, cotangent, mid, hidden, slope, expand_weight, reduce_weight, lines)
    if paired:
        sums.begin("a", plane_first([order.tie(expand_one)], sizes))
    advance()
    second_gradient = order.tie(second_gradient)
    layer_output, second_gradient, expand_two, bias_two = pl.pallas_call(
        last_reduce_kernel,
        name="reduce_two",
        cost_estimate=SMALL,
        grid=(half_steps,),
        in_specs=[whole(second), whole(cotangent), whole(mid), whole(mid)] + from_step(half_steps),
        out_specs=[whole(tokens)] + reduce_outs[1:],
        out_shape=(shape((rows, width), bf16),) + reduce_shapes[1:],
        scratch_shapes=[pltpu.VMEM((rows, width), f32)],
    )(second, cotangent, so_far, second_gradient, hidden, slope, expand_weight, reduce_weight)
    expand_two = order.tie(expand_two)
    if paired:
        sums.begin("b", plane_first([expand_two], sizes))
    advance()

    wide_shape = shape((rows, 3 * width), bf16)
    count = rows // BLOCK
    back_shapes = (
        shape((rows, width), bf16),
        shape((rows, width), f32),
        wide_shape,
        shape((rows, width), bf16),
        shape((count, 8, width), f32),
    )
    backs = ()
    for begin in range(count):

        def some(array):
            return pl.BlockSpec((BLOCK, array.shape[1]), lambda i, begin=begin: (begin, 0))

        def lead(size):
            return pl.BlockSpec(size, lambda i, begin=begin: (begin, 0, 0))

        backs = pl.pallas_call(
            back_kernel,
            name="back",
            cost_estimate=SMALL,
            grid=(1,),
            in_specs=[
                some(mid),
                some(mid),
                some(stream),
                some(cotangent),
                some(projected),
                lead((per_step,) + codes.shape[1:]),
                whole(lines),
                whole(output_weight),
                whole(project_weight),
            ]
            + [pl.BlockSpec(memory_space=pl.ANY)] * len(backs),
            out_specs=[some(array) for array in back_shapes[:4]] + [lead((1, 8, width))],
            out_shape=back_shapes,
            input_output_aliases={9 + k: k for k in range(len(backs))},
        )(
            order.tie(second_gradient),
            mid,
            stream,
            cotangent,
            projected,
            codes,
            lines,
            output_weight,
            project_weight,
            *backs,
        )
        backs = order.tie(*backs)
        advance()
    token_gradient, in_gradient, pieces, branch, block_sums = backs

    cut = 3 * width // 2
    narrow_block = width // 2
    project_gradient = pl.pallas_call(
        project_kernel,
        name="project",
        cost_estimate=SMALL,
        grid=(3 * width // narrow_block,),
        in_specs=[whole(first), pl.BlockSpec((rows, narrow_block), lambda i: (0, i))],
        out_specs=pl.BlockSpec((width, narrow_block), lambda i: (0, i)),
        out_shape=shape((width, 3 * width), f32),
    )(first, order.tie(pieces))
    project_gradient = order.tie(project_gradient)
    if paired:
        sums.begin("p", plane_first([project_gradient[:, :cut]], sizes))
        sums.begin("q", plane_first([project_gradient[:, cut:]], sizes))
    advance()
    heads_half, place_half = width // 2, places // 2
    top = heads_half + place_half + 32
    bias_rows = jnp.concatenate([bias_one, bias_two]).reshape(-1, width)
    mixed_inputs = (heads, order.tie(branch), in_gradient, codes, block_sums, bias_rows)
    mixed_shape = shape((2 * top, width), f32)
    mixed = pl.pallas_call(
        mixed_kernel,
        name="mixed",
        cost_estimate=SMALL,
        grid=(1,),
        in_specs=[whole(array) for array in mixed_inputs],
        out_specs=whole(mixed_shape),
        out_shape=mixed_shape,
    )(*mixed_inputs)
    mixed = order.tie(mixed)
    if paired:
        sums.begin("m", plane_first([mixed], sizes))
        advance()
        core = lax.axis_index("c")
        done = sums.results
        reduce_weight_gradient = done["w"]
        expand_weight_gradient, project_weight_gradient = done["ab"], done["pq"]
        output_weight_gradient, position_gradient, small = pl.pallas_call(
            divide_kernel,
            name="divide",
            in_specs=[pl.BlockSpec(memory_space=pltpu.SMEM)]
            + [pl.BlockSpec(memory_space=pltpu.VMEM)] * 2,
            out_specs=[pl.BlockSpec(memory_space=pltpu.VMEM)] * 3,
            out_shape=(
                shape((width, width), f32),
                shape((places, width), f32),
                shape((32, width), f32),
            ),
        )(jnp.reshape(core, (1,)), *done["m"])
    else:
        (
            reduce_weight_gradient,
            expand_weight_gradient,
            project_weight_gradient,
            mixed,
        ) = lax.psum(
            (
                reduce_weight_gradient,
                jnp.concatenate([expand_one, expand_two], axis=1),
                project_gradient,
                mixed,
            ),
            AXES,
        )
        mixed = mixed.reshape(2, top, width)
        output_weight_gradient = mixed[:, :heads_half].reshape(width, width)
        position_gradient = mixed[:, heads_half : top - 32].reshape(places, width)
        small = mixed[0, top - 32 :]
    (
        norm_one_gain_gradient,
        norm_one_shift_gradient,
        query_bias_gradient,
        value_bias_gradient,
        output_bias_gradient,
        norm_two_gain_gradient,
        norm_two_shift_gradient,
        reduce_bias_gradient,
    ) = (small[k] for k in range(8))
    expand_bias_gradient = small[8:12].reshape(-1)
    return (
        layer_output,
        token_gradient,
        position_gradient,
        norm_one_gain_gradient,
        norm_one_shift_gradient,
        project_weight_gradient,
        query_bias_gradient,
        value_bias_gradient,
        output_weight_gradient,
        output_bias_gradient,
        norm_two_gain_gradient,
        norm_two_shift_gradient,
        expand_weight_gradient,
        expand_bias_gradient,
        reduce_weight_gradient,
        reduce_bias_gradient,
    )


def solution(mesh):
    wide, narrow = mesh.shape["wide"], mesh.shape["narrow"]
    mesh = Mesh(mesh.devices.reshape(wide // 4, 2, 2, narrow), AXES)
    placed = (
        P(AXES, None),
        P(AXES, None),
        P(AXES),
        P(),
        P(),
        P(),
        P(),
        P(),
        P(),
        P(),
        P(),
        P(),
        P(),
        P(),
        P(),
        P(),
        P(),
        P(AXES, None),
    )
    return jax.shard_map(
        body,
        mesh=mesh,
        in_specs=placed,
        out_specs=(
            P(AXES, None),
            P(AXES, None),
            P(),
            P(),
            P(),
            P(),
            P(),
            P(),
            P(),
            P(),
            P(),
            P(),
            P(),
            P(),
            P(),
            P(),
        ),
        check_vma=False,
    )
```

```python
import itertools

import jax
import jax.numpy as jnp
from jax import lax
from jax.experimental import pallas as pl
from jax.experimental.pallas import tpu as pltpu
from jax.sharding import Mesh, PartitionSpec as P

HEADS = 12
PATCH_LO = 128
BLOCK = 256
FRONT = 512
WIDE = 512
PLAN = "|a|b|a|b|ab||paq+mbpaqbmapqbmpaqb*pmaqpbampqbmpqmpqqmm"

SMALL = pl.CostEstimate(flops=1, transcendentals=0, bytes_accessed=1)

epsilon = 1e-06
big_negative = -1e30
f32 = jnp.float32
bf16 = jnp.bfloat16


AXES = ("z", "y", "c", "x")
CHIPS_FIRST = ("z", "y", "x", "c")


def pairs(sizes, target):
    found = []
    for here in itertools.product(*(range(n) for n in sizes)):
        there = target(*here)
        if there is not None:
            found.append((flat(sizes, here), flat(sizes, there)))
    return found


def flat(sizes, place):
    index = 0
    for n, k in zip(sizes, place):
        index = index * n + k
    return index


def send(value, sizes, target):
    return lax.ppermute(value, AXES, pairs(sizes, target))


def across_core(z, y, c, x):
    return (z, y, 1 - c, x)


def plane_one(z, y, c, x):
    return (z, y, c, 1 - x) if c == 0 else (z, 1 - y, c, x)


def plane_two(z, y, c, x):
    return (z, 1 - y, c, x) if c == 0 else (z, y, c, 1 - x)


def ends_in(z, y, c, x):
    return {0: (1, y, c, x), 3: (2, y, c, x)}.get(z)


def middle(z, y, c, x):
    return {1: (2, y, c, x), 2: (1, y, c, x)}.get(z)


def ends_out(z, y, c, x):
    return {1: (0, y, c, x), 2: (3, y, c, x)}.get(z)


def half(value, index):
    rows = value.shape[0] // 2
    return lax.dynamic_slice_in_dim(value, index * rows, rows, 0)


def join(own, other, index):
    return jnp.concatenate(
        [jnp.where(index == 0, own, other), jnp.where(index == 0, other, own)], axis=0
    )


class Order:
    def __init__(self, token):
        self.token = token

    def tie(self, *values):
        *values, self.token = lax.optimization_barrier((*values, self.token))
        return values[0] if len(values) == 1 else tuple(values)


def plane_first(parts, sizes):
    z, y, c, x = (lax.axis_index(axis) for axis in AXES)
    first = jnp.where(c == 0, x, y)
    second = jnp.where(c == 0, y, x)
    other = sum(half(part, 1 - c) for part in parts)
    came = yield other, across_core
    value = sum(half(part, c) for part in parts) + came
    came = yield half(value, 1 - first), plane_one
    value = half(value, first) + came
    came = yield half(value, 1 - second), plane_two
    value = half(value, second) + came
    value = value + (yield value, ends_in)
    value = value + (yield value, middle)
    came = yield value, ends_out
    value = jnp.where((z == 0) | (z == 3), came, value)
    value = join(value, (yield value, plane_two), second)
    value = join(value, (yield value, plane_one), first)
    came = yield value, across_core
    return value, came


class Sums:
    def __init__(self, sizes, order):
        self.sizes, self.order = sizes, order
        self.steps, self.flying, self.results = {}, {}, {}

    def begin(self, name, steps):
        self.steps[name] = steps
        self.post(name, next(steps))

    def post(self, name, step):
        value, target = step
        if name == "m" and target is across_core and "ab" in self.results:
            value = after(value, self.results["ab"], self.results["w"])
        self.flying[name] = send(self.order.tie(value), self.sizes, target)

    def wait(self, *names):
        for name in names:
            came = self.order.tie(self.flying.pop(name))
            try:
                step = self.steps[name].send(came)
            except StopIteration as stop:
                self.results[name] = stop.value
            else:
                self.post(name, step)


def assemble(index, pairs, begin, rows, block):
    count = len(pairs)
    steps = rows // block
    lead = begin // block
    width = sum(own.shape[1] for own, _ in pairs)

    def kernel(where, *refs):
        mine = pl.program_id(0) == where[0]
        out = refs[-1]
        at = 0
        for own, other in zip(refs[:count], refs[count : 2 * count]):
            span = slice(at, at + own.shape[1])
            at += own.shape[1]

            @pl.when(mine)
            def _():
                out[:, span] = own[...]

            @pl.when(jnp.logical_not(mine))
            def _():
                out[:, span] = other[...]

    def own_map(h, i, where):
        return (lead + jnp.where(h == where[0], i, jnp.where(h == 0, 0, steps - 1)), 0)

    def other_map(h, i, where):
        return (lead + jnp.where(h == where[0], jnp.where(h == 0, 0, steps - 1), i), 0)

    return pl.pallas_call(
        kernel,
        name="assemble",
        grid_spec=pltpu.PrefetchScalarGridSpec(
            num_scalar_prefetch=1,
            grid=(2, steps),
            in_specs=[pl.BlockSpec((block, own.shape[1]), own_map) for own, _ in pairs]
            + [pl.BlockSpec((block, own.shape[1]), other_map) for own, _ in pairs],
            out_specs=pl.BlockSpec((block, width), lambda h, i, where: (h * steps + i, 0)),
        ),
        out_shape=jax.ShapeDtypeStruct((2 * rows, width), f32),
    )(jnp.reshape(index, (1,)), *(own for own, _ in pairs), *(other for _, other in pairs))


def after(value, *others):
    anywhere = pl.BlockSpec(memory_space=pl.ANY)
    return pl.pallas_call(
        lambda *refs: None,
        name="after",
        in_specs=[anywhere] * (1 + len(others)),
        out_specs=anywhere,
        out_shape=jax.ShapeDtypeStruct(value.shape, value.dtype),
        input_output_aliases={0: 0},
    )(value, *others)


def copy_kernel(source, target):
    target[...] = source[...]


def copied(array, block):
    spec = pl.BlockSpec((block, array.shape[1]), lambda i: (i, 0))
    return pl.pallas_call(
        copy_kernel,
        name="copied",
        grid=(array.shape[0] // block,),
        in_specs=[spec],
        out_specs=spec,
        out_shape=jax.ShapeDtypeStruct(array.shape, array.dtype),
    )(array)


def divide_kernel(where, own, other, weights, places, small):
    heads_half, place_half = weights.shape[0] // 2, places.shape[0] // 2
    top = own.shape[0]

    def fill(low, high):
        weights[:heads_half, :] = low[:heads_half, :]
        weights[heads_half:, :] = high[:heads_half, :]
        places[:place_half, :] = low[heads_half : heads_half + place_half, :]
        places[place_half:, :] = high[heads_half : heads_half + place_half, :]
        small[...] = low[top - 32 :, :]

    @pl.when(where[0] == 0)
    def _():
        fill(own, other)

    @pl.when(where[0] != 0)
    def _():
        fill(other, own)


def mm(first, second):
    return lax.dot_general(first, second, (((1,), (0,)), ((), ())), preferred_element_type=f32)


def mm_nt(first, second):
    return lax.dot_general(first, second, (((1,), (1,)), ((), ())), preferred_element_type=f32)


def mm_tn(first, second):
    return lax.dot_general(first, second, (((0,), (0,)), ((), ())), preferred_element_type=f32)


def normalize(stream):
    centre = stream - jnp.mean(stream, axis=-1, keepdims=True)
    inverse = lax.rsqrt(jnp.mean(centre * centre, axis=-1, keepdims=True) + epsilon)
    return centre * inverse, inverse


def norm_backward(upstream, normed, inverse, gain):
    scaled = upstream * gain
    inner = jnp.mean(scaled * normed, axis=-1, keepdims=True)
    return inverse * (scaled - jnp.mean(scaled, axis=-1, keepdims=True) - normed * inner)


def column_sum(value):
    return jnp.sum(value, axis=0, keepdims=True)


def two_heads(pair, low_lanes):
    zero = jnp.zeros_like(pair)
    return jnp.concatenate(
        [jnp.where(low_lanes, pair, zero), jnp.where(low_lanes, zero, pair)], axis=0
    )


def all_probs(queries, keys, same):
    scores = [mm_nt(q, k) for q, k in zip(queries, keys)]
    scores = [jnp.where(same, one, big_negative) for one in scores]
    tops = [jnp.max(one, axis=-1, keepdims=True) for one in scores]
    exponents = [jnp.exp(one - top) for one, top in zip(scores, tops)]
    totals = [jnp.sum(one, axis=-1, keepdims=True) for one in exponents]
    return [one * (1.0 / total) for one, total in zip(exponents, totals)]


def row_of(codes, which):
    return jnp.concatenate([codes[k][which : which + 1] for k in range(codes.shape[0])], axis=1)


def chosen_places(codes, places):
    row = row_of(codes, 0)
    numbers = lax.broadcasted_iota(jnp.int32, (places, row.shape[1]), 0)
    return (numbers == row).astype(bf16)


def same_sample(codes, g):
    numbers = lax.broadcasted_iota(jnp.int32, (16, codes.shape[2]), 0)
    member = (numbers == codes[g][1:2]).astype(bf16)
    same = mm_tn(member, member)
    return jnp.concatenate([same, same], axis=0) > 0.5


def front_kernel(
    tokens,
    codes,
    table,
    lines,
    project_weight,
    output_weight,
    stream_out,
    first_out,
    projected_out,
    heads_out,
    mid_out,
    second_out,
):
    rows, width = tokens.shape
    group = codes.shape[2]
    scale = (width // HEADS) ** (-0.5)
    chosen = chosen_places(codes, table.shape[0])
    stream = tokens[...].astype(f32) + mm_tn(chosen, table[...])
    stream_out[...] = stream
    normed, _ = normalize(stream)
    first = (normed * lines[0:1] + lines[1:2]).astype(bf16)
    first_out[...] = first
    joined_bias = jnp.concatenate([lines[6:7], jnp.zeros((1, width), f32), lines[7:8]], axis=1)
    projected_out[...] = (mm(first, project_weight[...]) + joined_bias).astype(bf16)
    low_lanes = lax.broadcasted_iota(jnp.int32, (group, 128), 1) < 64
    for g in range(rows // group):
        span = slice(g * group, (g + 1) * group)
        same = same_sample(codes, g)
        here = [slice(j * 128, (j + 1) * 128) for j in range(3 * width // 128)]
        count = width // 128
        columns = [projected_out[span, one] for one in here]
        queries = [two_heads(one * bf16(scale), low_lanes) for one in columns[:count]]
        probs = all_probs(queries, columns[count : 2 * count], same)
        both = [mm(p.astype(bf16), v) for p, v in zip(probs, columns[2 * count :])]
        for j in range(count):
            heads_out[span, here[j]] = jnp.where(
                low_lanes, both[j][:group], both[j][group:]
            ).astype(bf16)
    mid = stream + (mm(heads_out[...], output_weight[...]) + lines[4:5])
    mid_out[...] = mid
    normed, _ = normalize(mid)
    second_out[...] = (normed * lines[2:3] + lines[3:4]).astype(bf16)


def expand_kernel(
    second, cotangent, expand_weight, expand_bias, hidden_out, slope_out, reduce_gradient
):
    before = mm(second[...], expand_weight[...]) + expand_bias[...]
    below = 0.5 * (1.0 + lax.erf(before * (0.5**0.5)))
    density = jnp.exp(-0.5 * before * before) * 0.3989422804014327
    hidden = (before * below).astype(bf16)
    hidden_out[...] = hidden
    slope_out[...] = (below + before * density).astype(bf16)
    reduce_gradient[...] = mm_tn(hidden, cotangent[...])


def reduce_kernel(
    second,
    cotangent,
    before_total,
    before_gradient,
    hidden,
    slope,
    expand_weight,
    reduce_weight,
    lines,
    total,
    second_gradient,
    expand_gradient,
    bias_gradient,
    *,
    fresh,
):
    step = pl.program_id(0)
    gradient = mm_nt(cotangent[...], reduce_weight[...])
    low = (gradient * slope[...].astype(f32)).astype(bf16)
    bias_gradient[0] = column_sum(low.astype(f32))
    expand_gradient[...] = mm_tn(second[...], low)
    back = mm_nt(low, expand_weight[...])
    ahead = mm(hidden[...], reduce_weight[...])

    @pl.when(step == 0)
    def _():
        if fresh:
            second_gradient[...] = back
            total[...] = before_total[...] + lines[5:6] + ahead
        else:
            second_gradient[...] = before_gradient[...] + back
            total[...] = before_total[...] + ahead

    @pl.when(step > 0)
    def _():
        second_gradient[...] += back
        total[...] += ahead


def first_reduce_kernel(
    second, cotangent, mid, hidden, slope, expand_weight, reduce_weight, lines, *outs
):
    reduce_kernel(
        second, cotangent, mid, None, hidden, slope, expand_weight, reduce_weight, lines,
        *outs, fresh=True,
    )


def last_reduce_kernel(
    second, cotangent, before_total, before_gradient, hidden, slope, expand_weight,
    reduce_weight, layer_out, second_gradient, expand_gradient, bias_gradient, total,
):
    reduce_kernel(
        second, cotangent, before_total, before_gradient, hidden, slope, expand_weight,
        reduce_weight, None, total, second_gradient, expand_gradient, bias_gradient,
        fresh=False,
    )

    @pl.when(pl.program_id(0) == pl.num_programs(0) - 1)
    def _():
        layer_out[...] = total[...].astype(bf16)


def back_kernel(
    second_gradient,
    mid,
    stream,
    cotangent,
    projected,
    codes,
    lines,
    output_weight,
    project_weight,
    *rest,
):
    token_gradient, in_gradient_out, pieces, branch_out, sums = rest[-5:]
    rows, width = stream.shape
    group = codes.shape[2]
    scale = (width // HEADS) ** (-0.5)
    upstream = second_gradient[...]
    out_gradient = cotangent[...].astype(f32)
    normed, inverse = normalize(mid[...])
    two_gain_gradient = column_sum(upstream * normed)
    two_shift_gradient = column_sum(upstream)
    mid_gradient = out_gradient + norm_backward(upstream, normed, inverse, lines[2:3])
    branch = mid_gradient.astype(bf16)
    branch_out[...] = branch
    bias_gradient = column_sum(branch.astype(f32))
    heads_gradient = mm_nt(branch, output_weight[...]).astype(bf16)
    low_lanes = lax.broadcasted_iota(jnp.int32, (group, 128), 1) < 64
    for g in range(rows // group):
        span = slice(g * group, (g + 1) * group)
        same = same_sample(codes, g)
        here = [slice(j * 128, (j + 1) * 128) for j in range(3 * width // 128)]
        count = width // 128
        columns = [projected[span, one] for one in here]
        queries = [two_heads(one * bf16(scale), low_lanes) for one in columns[:count]]
        keys, values = columns[count : 2 * count], columns[2 * count :]
        uppers = [two_heads(heads_gradient[span, one], low_lanes) for one in here[:count]]
        probs = all_probs(queries, keys, same)
        weights = [mm_nt(upper, v) for upper, v in zip(uppers, values)]
        inner = [jnp.sum(w * p, axis=-1, keepdims=True) for w, p in zip(weights, probs)]
        scores = [(p * (w - n)).astype(bf16) for p, w, n in zip(probs, weights, inner)]
        for_queries = [mm(one, k) for one, k in zip(scores, keys)]
        for_keys = [mm_tn(one, q) for one, q in zip(scores, queries)]
        for_values = [mm_tn(p.astype(bf16), upper) for p, upper in zip(probs, uppers)]
        for j in range(count):
            both = for_queries[j]
            pieces[span, here[j]] = (
                jnp.where(low_lanes, both[:group], both[group:]) * scale
            ).astype(bf16)
            pieces[span, here[count + j]] = for_keys[j].astype(bf16)
            pieces[span, here[2 * count + j]] = for_values[j].astype(bf16)
    upstream = mm_nt(pieces[...], project_weight[...])
    normed, inverse = normalize(stream[...])
    in_gradient = mid_gradient + norm_backward(upstream, normed, inverse, lines[0:1])
    in_gradient_out[...] = in_gradient
    token_gradient[...] = in_gradient.astype(bf16)
    sums[0] = jnp.concatenate(
        [
            column_sum(upstream * normed),
            column_sum(upstream),
            column_sum(pieces[:, :width].astype(f32)),
            column_sum(pieces[:, 2 * width :].astype(f32)),
            bias_gradient,
            two_gain_gradient,
            two_shift_gradient,
            column_sum(out_gradient),
        ],
        axis=0,
    )


def project_kernel(first, pieces, *rest):
    project_gradient = rest[-1]
    project_gradient[...] = mm_tn(first[...], pieces[...])


def mixed_kernel(heads, branch, in_gradient, codes, sums, expand_bias_gradient, *rest):
    mixed = rest[-1]
    width = heads.shape[1]
    top = mixed.shape[0] // 2
    heads_half = width // 2
    place_half = top - heads_half - 32
    both = mm_tn(heads[...], branch[...])
    mixed[:heads_half, :] = both[:heads_half]
    mixed[top : top + heads_half, :] = both[heads_half:]
    high = in_gradient[...].astype(bf16)
    low = (in_gradient[...] - high.astype(f32)).astype(bf16)
    chosen = chosen_places(codes, 2 * place_half)
    both = mm(chosen, high) + mm(chosen, low)
    mixed[heads_half : heads_half + place_half, :] = both[:place_half]
    mixed[top + heads_half : top + heads_half + place_half, :] = both[place_half:]
    mixed[top - 32 : top, :] = jnp.zeros((32, width), f32)
    mixed[2 * top - 32 :, :] = jnp.zeros((32, width), f32)
    total = sums[0]
    for k in range(1, sums.shape[0]):
        total = total + sums[k]
    mixed[top - 32 : top - 24, :] = total
    mixed[top - 24 : top - 20, :] = expand_bias_gradient[...]


def lines_kernel(*refs):
    *vectors, last, lines, bias_row = refs
    for k, vector in enumerate(vectors):
        lines[k : k + 1, :] = vector[...].astype(f32).reshape(1, -1)
    bias_row[...] = last[...].astype(f32).reshape(1, -1)


def whole(array):
    return pl.BlockSpec(array.shape, lambda i: (0,) * array.ndim)


def row_block(array):
    return pl.BlockSpec((FRONT, array.shape[1]), lambda i: (i, 0))


def lead_block(array, count=1):
    return pl.BlockSpec((count,) + array.shape[1:], lambda i: (i, 0, 0))


def shape(dims, kind):
    return jax.ShapeDtypeStruct(dims, kind)


def body(
    tokens,
    kept_patches,
    resolution,
    position_table,
    norm_one_gain,
    norm_one_shift,
    project_weight,
    query_bias,
    value_bias,
    output_weight,
    output_bias,
    norm_two_gain,
    norm_two_shift,
    expand_weight,
    expand_bias,
    reduce_weight,
    reduce_bias,
    cotangent,
):
    groups, group_rows = kept_patches.shape
    rows, width = tokens.shape
    hidden_width = expand_weight.shape[1]
    places = position_table.shape[0]
    per_step = BLOCK // group_rows
    fine_grid = resolution[:, None] == 1
    place = jnp.where(fine_grid, PATCH_LO + kept_patches, kept_patches % PATCH_LO)
    sample = jnp.where(fine_grid, 0, kept_patches // PATCH_LO)
    codes = jnp.stack([place, sample], axis=1)
    vectors = (
        norm_one_gain,
        norm_one_shift,
        norm_two_gain,
        norm_two_shift,
        output_bias,
        reduce_bias,
        query_bias,
        value_bias,
        expand_bias,
    )
    lines, bias_row = pl.pallas_call(
        lines_kernel,
        name="lines",
        in_specs=[pl.BlockSpec(memory_space=pltpu.VMEM)] * len(vectors),
        out_specs=[pl.BlockSpec(memory_space=pltpu.VMEM)] * 2,
        out_shape=(shape((8, width), f32), shape((1, hidden_width), f32)),
    )(*vectors)
    front_shapes = (
        shape((rows, width), f32),
        shape((rows, width), bf16),
        shape((rows, 3 * width), bf16),
        shape((rows, width), bf16),
        shape((rows, width), f32),
        shape((rows, width), bf16),
    )
    fixed = (position_table, lines, project_weight, output_weight)
    stream, first, projected, heads, mid, second = pl.pallas_call(
        front_kernel,
        name="front",
        grid=(rows // FRONT,),
        in_specs=[row_block(tokens), lead_block(codes, FRONT // group_rows)]
        + [whole(array) for array in fixed],
        out_specs=[row_block(array) for array in front_shapes],
        out_shape=front_shapes,
    )(tokens, codes, *fixed)

    columns = pl.BlockSpec((width, WIDE), lambda i: (0, i))
    tall = pl.BlockSpec((rows, WIDE), lambda i: (0, i))
    low_lines = pl.BlockSpec((WIDE, width), lambda i: (i, 0))
    hidden, slope, reduce_weight_gradient = pl.pallas_call(
        expand_kernel,
        name="expand",
        grid=(hidden_width // WIDE,),
        in_specs=[
            whole(second),
            whole(cotangent),
            columns,
            pl.BlockSpec((1, WIDE), lambda i: (0, i)),
        ],
        out_specs=[tall, tall, low_lines],
        out_shape=(
            shape((rows, hidden_width), bf16),
            shape((rows, hidden_width), bf16),
            shape((hidden_width, width), f32),
        ),
    )(second, cotangent, expand_weight, bias_row)

    sizes = tuple(lax.axis_size(axis) for axis in AXES)
    paired = sizes == (4, 2, 2, 2)
    order = Order(codes)
    sums = Sums(sizes, order)
    reduce_weight_gradient, second = order.tie(reduce_weight_gradient, second)
    if paired:
        reduce_weight_gradient = lax.psum_scatter(
            reduce_weight_gradient, CHIPS_FIRST, scatter_dimension=0, tiled=True
        )
    plan = iter(PLAN)

    def advance():
        for name in plan:
            if name == "|":
                break
            if name == "+" and paired:
                sums.results["w"] = lax.all_gather(
                    order.tie(reduce_weight_gradient), CHIPS_FIRST, axis=0, tiled=True
                )
            elif name == "*" and paired:
                sums.results["w"] = order.tie(copied(order.tie(sums.results["w"]), 3 * WIDE // 2))
            elif paired:
                sums.wait(name)
                for both in ("ab", "pq"):
                    if both not in sums.results and all(one in sums.results for one in both):
                        pairs = tuple(order.tie(*sums.results[one]) for one in both)
                        sums.results[both] = order.tie(
                            assemble(lax.axis_index("c"), pairs, 0, width // 2, width // 4)
                        )

    half_steps = hidden_width // WIDE // 2
    part = hidden_width // 2
    reduce_shapes = (
        shape((rows, width), f32),
        shape((rows, width), f32),
        shape((width, part), f32),
        shape((half_steps, 1, WIDE), f32),
    )

    def from_step(begin):
        return [
            pl.BlockSpec((rows, WIDE), lambda i: (0, i + begin)),
            pl.BlockSpec((rows, WIDE), lambda i: (0, i + begin)),
            pl.BlockSpec((width, WIDE), lambda i: (0, i + begin)),
            pl.BlockSpec((WIDE, width), lambda i: (i + begin, 0)),
        ]

    reduce_outs = [whole(mid), whole(mid), columns, pl.BlockSpec((1, 1, WIDE), lambda i: (i, 0, 0))]
    so_far, second_gradient, expand_one, bias_one = pl.pallas_call(
        first_reduce_kernel,
        name="reduce_one",
        cost_estimate=SMALL,
        grid=(half_steps,),
        in_specs=[whole(second), whole(cotangent), whole(mid)] + from_step(0) + [whole(lines)],
        out_specs=reduce_outs,
        out_shape=reduce_shapes,
    )(second, cotangent, mid, hidden, slope, expand_weight, reduce_weight, lines)
    if paired:
        sums.begin("a", plane_first([order.tie(expand_one)], sizes))
    advance()
    second_gradient = order.tie(second_gradient)
    layer_output, second_gradient, expand_two, bias_two = pl.pallas_call(
        last_reduce_kernel,
        name="reduce_two",
        cost_estimate=SMALL,
        grid=(half_steps,),
        in_specs=[whole(second), whole(cotangent), whole(mid), whole(mid)] + from_step(half_steps),
        out_specs=[whole(tokens)] + reduce_outs[1:],
        out_shape=(shape((rows, width), bf16),) + reduce_shapes[1:],
        scratch_shapes=[pltpu.VMEM((rows, width), f32)],
    )(second, cotangent, so_far, second_gradient, hidden, slope, expand_weight, reduce_weight)
    expand_two = order.tie(expand_two)
    if paired:
        sums.begin("b", plane_first([expand_two], sizes))
    advance()

    wide_shape = shape((rows, 3 * width), bf16)
    count = rows // BLOCK
    back_shapes = (
        shape((rows, width), bf16),
        shape((rows, width), f32),
        wide_shape,
        shape((rows, width), bf16),
        shape((count, 8, width), f32),
    )
    backs = ()
    for begin in range(count):

        def some(array):
            return pl.BlockSpec((BLOCK, array.shape[1]), lambda i, begin=begin: (begin, 0))

        def lead(size):
            return pl.BlockSpec(size, lambda i, begin=begin: (begin, 0, 0))

        backs = pl.pallas_call(
            back_kernel,
            name="back",
            cost_estimate=SMALL,
            grid=(1,),
            in_specs=[
                some(mid),
                some(mid),
                some(stream),
                some(cotangent),
                some(projected),
                lead((per_step,) + codes.shape[1:]),
                whole(lines),
                whole(output_weight),
                whole(project_weight),
            ]
            + [pl.BlockSpec(memory_space=pl.ANY)] * len(backs),
            out_specs=[some(array) for array in back_shapes[:4]] + [lead((1, 8, width))],
            out_shape=back_shapes,
            input_output_aliases={9 + k: k for k in range(len(backs))},
        )(
            order.tie(second_gradient),
            mid,
            stream,
            cotangent,
            projected,
            codes,
            lines,
            output_weight,
            project_weight,
            *backs,
        )
        backs = order.tie(*backs)
        advance()
    token_gradient, in_gradient, pieces, branch, block_sums = backs

    cut = 3 * width // 2
    narrow_block = width // 2
    project_gradient = pl.pallas_call(
        project_kernel,
        name="project",
        cost_estimate=SMALL,
        grid=(3 * width // narrow_block,),
        in_specs=[whole(first), pl.BlockSpec((rows, narrow_block), lambda i: (0, i))],
        out_specs=pl.BlockSpec((width, narrow_block), lambda i: (0, i)),
        out_shape=shape((width, 3 * width), f32),
    )(first, order.tie(pieces))
    project_gradient = order.tie(project_gradient)
    if paired:
        sums.begin("p", plane_first([project_gradient[:, :cut]], sizes))
        sums.begin("q", plane_first([project_gradient[:, cut:]], sizes))
    advance()
    heads_half, place_half = width // 2, places // 2
    top = heads_half + place_half + 32
    bias_rows = jnp.concatenate([bias_one, bias_two]).reshape(-1, width)
    mixed_inputs = (heads, order.tie(branch), in_gradient, codes, block_sums, bias_rows)
    mixed_shape = shape((2 * top, width), f32)
    mixed = pl.pallas_call(
        mixed_kernel,
        name="mixed",
        cost_estimate=SMALL,
        grid=(1,),
        in_specs=[whole(array) for array in mixed_inputs],
        out_specs=whole(mixed_shape),
        out_shape=mixed_shape,
    )(*mixed_inputs)
    mixed = order.tie(mixed)
    if paired:
        sums.begin("m", plane_first([mixed], sizes))
        advance()
        core = lax.axis_index("c")
        done = sums.results
        reduce_weight_gradient = done["w"]
        expand_weight_gradient, project_weight_gradient = done["ab"], done["pq"]
        output_weight_gradient, position_gradient, small = pl.pallas_call(
            divide_kernel,
            name="divide",
            in_specs=[pl.BlockSpec(memory_space=pltpu.SMEM)]
            + [pl.BlockSpec(memory_space=pltpu.VMEM)] * 2,
            out_specs=[pl.BlockSpec(memory_space=pltpu.VMEM)] * 3,
            out_shape=(
                shape((width, width), f32),
                shape((places, width), f32),
                shape((32, width), f32),
            ),
        )(jnp.reshape(core, (1,)), *done["m"])
    else:
        (
            reduce_weight_gradient,
            expand_weight_gradient,
            project_weight_gradient,
            mixed,
        ) = lax.psum(
            (
                reduce_weight_gradient,
                jnp.concatenate([expand_one, expand_two], axis=1),
                project_gradient,
                mixed,
            ),
            AXES,
        )
        mixed = mixed.reshape(2, top, width)
        output_weight_gradient = mixed[:, :heads_half].reshape(width, width)
        position_gradient = mixed[:, heads_half : top - 32].reshape(places, width)
        small = mixed[0, top - 32 :]
    (
        norm_one_gain_gradient,
        norm_one_shift_gradient,
        query_bias_gradient,
        value_bias_gradient,
        output_bias_gradient,
        norm_two_gain_gradient,
        norm_two_shift_gradient,
        reduce_bias_gradient,
    ) = (small[k] for k in range(8))
    expand_bias_gradient = small[8:12].reshape(-1)
    return (
        layer_output,
        token_gradient,
        position_gradient,
        norm_one_gain_gradient,
        norm_one_shift_gradient,
        project_weight_gradient,
        query_bias_gradient,
        value_bias_gradient,
        output_weight_gradient,
        output_bias_gradient,
        norm_two_gain_gradient,
        norm_two_shift_gradient,
        expand_weight_gradient,
        expand_bias_gradient,
        reduce_weight_gradient,
        reduce_bias_gradient,
    )


def solution(mesh):
    wide, narrow = mesh.shape["wide"], mesh.shape["narrow"]
    mesh = Mesh(mesh.devices.reshape(wide // 4, 2, 2, narrow), AXES)
    placed = (
        P(AXES, None),
        P(AXES, None),
        P(AXES),
        P(),
        P(),
        P(),
        P(),
        P(),
        P(),
        P(),
        P(),
        P(),
        P(),
        P(),
        P(),
        P(),
        P(),
        P(AXES, None),
    )
    return jax.shard_map(
        body,
        mesh=mesh,
        in_specs=placed,
        out_specs=(
            P(AXES, None),
            P(AXES, None),
            P(),
            P(),
            P(),
            P(),
            P(),
            P(),
            P(),
            P(),
            P(),
            P(),
            P(),
            P(),
            P(),
            P(),
        ),
        check_vma=False,
    )
```
